32 devices in a mesh: frame: 2 (over x), depth: 4 (over z), row: 4 (over y, core).
Axes of the slice: x: 2, y: 2, z: 4, core: 2. Of those that a mesh axis runs over, the one named last changes fastest.
Arguments:
- volume: bfloat16 [4, 2, 8, 18432], P('depth', 'frame', 'row'), may hold values from -6 to 6
- point_spread: bfloat16 [4, 576, 25, 144], P('depth', 'frame', None, 'row'), may hold values from -0.046875 to 0.046875
- region_map: int32 [8, 128], replicated, may hold values from 0 to 3
- measured: bfloat16 [2, 8, 18432], P('frame', 'row', 'depth'), may hold values from -6 to 6
- pixel_weight: int32 [2, 8, 18432], P('frame', 'row', 'depth'), may hold values 0 or 1
Outputs:
- camera: float32 [2, 8, 18432], P('frame', 'row', 'depth')
- residual: float32 [2, 8, 18432], P('frame', 'row', 'depth')
The draws below stay inside these ranges and needn't reach their ends.
Inputs may be any that keep to these rules, and one draw needn't show every extreme that they name: `region_map`: the block that serves each lenslet.
All inputs are finite; a program needn't handle non-finite values. No bound on the sum of `pixel_weight` on one device may be relied on, other than what follows from the above.
Results may differ from the reference program's by a relative error of at most 0.0003.
Values may be sent and summed in bfloat16 or wider, within the bound.
A program may use at most 64 MiB of HBM per device.

```python
import jax
import jax.numpy as jnp
from jax import lax

PHASES = 144
BLOCKS = 4
TAP_SIDE = 5
LCOLS = 128
LROWS = 8
FRAMES = 2
DEPTHS = 4


def plant(array, key, smallest, largest):
    index_at = [jax.random.randint(jax.random.fold_in(key, axis), (), 0, length) for axis, length in enumerate(array.shape)]
    longest = array.shape.index(max(array.shape))
    beside = index_at[:longest] + [(index_at[longest] + 1) % array.shape[longest]] + index_at[longest + 1:]
    return array.at[tuple(index_at)].set(smallest).at[tuple(beside)].set(largest)


def shard_levels(stream_key, extent, shards, least, largest):
    loudness = 1.0
    for axis_at, shards_of in shards:
        steps = jax.random.uniform(jax.random.fold_in(jax.random.fold_in(stream_key, 6), axis_at), (shards_of,), jnp.float32, least / len(shards), largest / len(shards))
        loudness = loudness * jnp.repeat(jnp.exp(steps), extent[axis_at] // shards_of).reshape((-1,) + (1,) * (len(extent) - 1 - axis_at))
    return loudness


def gaussian(stream_key, shape, width, reach, cuts=(), kind=jnp.bfloat16):
    result = width * jax.random.normal(stream_key, shape, jnp.float32)
    if cuts:
        result = result * shard_levels(stream_key, shape, cuts, -0.22, 0.18)
    return jnp.clip(result, -reach, reach).astype(kind)


def setup_inputs(seed: int = 0) -> dict:
    streams_of = jax.random.split(jax.random.key(seed), 6)
    return {
        "volume": gaussian(streams_of[0], (DEPTHS, FRAMES, LROWS, LCOLS * PHASES), 1.0, 6.0, ((0, 4), (1, 2), (2, 4))),
        "point_spread": gaussian(streams_of[1], (DEPTHS, BLOCKS * PHASES, TAP_SIDE * TAP_SIDE, PHASES), (TAP_SIDE * TAP_SIDE * PHASES * DEPTHS) ** -0.5, 0.046875, ((0, 4), (1, 2), (3, 4))),
        "region_map": plant(jax.random.randint(streams_of[2], (LROWS, LCOLS), 0, BLOCKS), jax.random.fold_in(streams_of[2], 1), 0, BLOCKS - 1).astype(jnp.int32),
        "measured": gaussian(streams_of[3], (FRAMES, LROWS, LCOLS * PHASES), 1.0, 6.0, ((0, 2), (1, 4), (2, 4))),
        "pixel_weight": plant((jax.random.randint(streams_of[4], (FRAMES, LROWS, LCOLS * PHASES), 0, 4) < 3).astype(jnp.int32), jax.random.fold_in(streams_of[4], 1), 0, 1),
    }


def reference(volume, point_spread, region_map, measured, pixel_weight):
    tap_reach = TAP_SIDE // 2
    block_ids = jnp.arange(BLOCKS, dtype=jnp.int32)
    onehot = (region_map[:, :, None] == block_ids[None, None, :]).astype(jnp.float32)
    spread_all = point_spread.astype(jnp.float32)
    volume_split = volume.reshape(DEPTHS, FRAMES, LROWS, LCOLS, PHASES)

    def one_frame(planes):
        running = jnp.zeros((LROWS * LCOLS, PHASES), jnp.float32)
        for depth in range(DEPTHS):
            plane_now = planes[depth].astype(jnp.float32)
            expanded = (plane_now[:, :, None, :] * onehot[:, :, :, None]).reshape(LROWS, LCOLS, BLOCKS * PHASES)
            padded = jnp.pad(expanded, ((tap_reach, tap_reach), (tap_reach, tap_reach), (0, 0)))
            for tap_row in range(TAP_SIDE):
                for tap_col in range(TAP_SIDE):
                    first_row = 2 * tap_reach - tap_row
                    first_col = 2 * tap_reach - tap_col
                    shifted = padded[first_row:first_row + LROWS, first_col:first_col + LCOLS, :]
                    running = running + jnp.dot(shifted.reshape(LROWS * LCOLS, BLOCKS * PHASES),
                                                spread_all[depth, :, tap_row * TAP_SIDE + tap_col, :],
                                                precision=lax.Precision.HIGHEST)
        return running.reshape(LROWS, LCOLS * PHASES)

    camera = lax.map(one_frame, jnp.swapaxes(volume_split, 0, 1))
    residual = pixel_weight.astype(jnp.float32) * (camera - measured.astype(jnp.float32))
    return (camera, residual)
```

```python
import functools

import jax
import jax.numpy as jnp
from jax import lax
from jax.experimental import pallas as pl
from jax.experimental.pallas import tpu as pltpu
from jax.sharding import PartitionSpec as P

PHASES = 144
BLOCKS = 4
TAP_SIDE = 5


def build_taps(planes, region_rows):
    tap_reach = TAP_SIDE // 2
    frames, row_count, merged = planes.shape
    col_count = merged // PHASES
    split_planes = planes.reshape(frames, row_count, col_count, PHASES)
    block_ids = jnp.arange(BLOCKS, dtype=jnp.int32)
    onehot = (region_rows[:, :, None] == block_ids[None, None, :]).astype(jnp.bfloat16)
    expanded = (split_planes[:, :, :, None, :] * onehot[None, :, :, :, None]).reshape(
        frames, row_count, col_count, BLOCKS * PHASES
    )
    return jnp.pad(expanded, ((0, 0), (0, 0), (tap_reach, tap_reach), (0, 0)))


def project(padded, spread_local, out_rows):
    tap_reach = TAP_SIDE // 2
    frames, ext_rows, ext_cols, _ = padded.shape
    col_count = ext_cols - 2 * tap_reach
    out_width = spread_local.shape[2]
    zero_start = jnp.zeros((frames * out_rows * col_count, out_width), jnp.float32)
    running = zero_start
    spread_slab = lax.all_gather(spread_local, "frame", axis=0, tiled=True)
    piece_rows = spread_slab.shape[0]
    flat_cols = padded.reshape(frames * ext_rows * ext_cols, piece_rows)
    for tap_row in range(TAP_SIDE):
        row_taps = spread_slab[:, tap_row * TAP_SIDE : (tap_row + 1) * TAP_SIDE, :].reshape(
            piece_rows, TAP_SIDE * out_width
        )
        product = jnp.dot(flat_cols, row_taps, preferred_element_type=jnp.float32)
        product = product.reshape(frames, ext_rows, ext_cols, TAP_SIDE, out_width)
        first_row = 2 * tap_reach - tap_row
        for tap_col in range(TAP_SIDE):
            first_col = 2 * tap_reach - tap_col
            shifted = product[
                :, first_row : first_row + out_rows, first_col : first_col + col_count, tap_col, :
            ]
            running = running + shifted.reshape(frames * out_rows * col_count, out_width)
    partial_value = running.reshape(frames, out_rows, col_count * out_width)
    return lax.psum_scatter(partial_value, "depth", scatter_dimension=2, tiled=True)


def plain_body(volume, point_spread, region_map, measured, pixel_weight):
    tap_reach = TAP_SIDE // 2
    planes = volume[0]
    row_count = planes.shape[1]
    region_padded = jnp.pad(region_map, ((tap_reach, tap_reach), (0, 0)), constant_values=-1)
    all_rows = lax.all_gather(planes, "row", axis=1, tiled=True)
    extended = jnp.pad(all_rows, ((0, 0), (tap_reach, tap_reach), (0, 0)))
    padded = build_taps(extended, region_padded)
    piece_width = point_spread.shape[3]
    partial_value = project(padded, point_spread[0], all_rows.shape[1])
    frames, total_rows, merged = partial_value.shape
    split_partial = partial_value.reshape(frames, total_rows, merged // piece_width, piece_width)
    returned = lax.all_to_all(split_partial, "row", split_axis=1, concat_axis=3, tiled=True)
    camera = returned.reshape(frames, row_count, returned.shape[2] * returned.shape[3])
    residual = pixel_weight.astype(jnp.float32) * (camera - measured.astype(jnp.float32))
    return (camera, residual)


def round_up(value, step):
    return (value + step - 1) // step * step


def remote(src, dst, send_sem, recv_sem, device):
    return pltpu.make_async_remote_copy(
        src_ref=src, dst_ref=dst, send_sem=send_sem, recv_sem=recv_sem,
        device_id=device, device_id_type=pl.DeviceIdType.MESH,
    )


def kernel(frames, depths, row_shards, vin, w_hbm, region, cam, vol, wraw, wflat, xmask, part, xrecv, zsend,
           zrecv, yred, fin, w_sem, g_send, g_recv, x_send, x_recv, z_send, z_recv, y_send, y_recv):
    reach = TAP_SIDE // 2
    rows_here, phases, cols = vin.shape
    rows = rows_here * row_shards
    taps, width, depth_rows = w_hbm.shape
    blocks_here = depth_rows // phases
    stride = wflat.shape[0] // TAP_SIDE
    qpad = part.shape[3]
    col_share = cols // depths
    quads = rows // depths
    me_f, me_d, me_r = lax.axis_index("frame"), lax.axis_index("depth"), lax.axis_index("row")
    other_f = 1 - me_f
    core_r = me_r + 1 - 2 * lax.rem(me_r, 2)
    far_r = lax.rem(me_r + 2, row_shards)
    far_core_r = far_r + 1 - 2 * lax.rem(far_r, 2)

    w_copy = pltpu.make_async_copy(w_hbm, wraw, w_sem)
    w_copy.start()

    x_dev = (other_f, me_d, me_r)
    core_dev = (me_f, me_d, core_r)
    far_dev = (me_f, me_d, far_r)
    diag_dev = (other_f, me_d, far_r)
    partners = [x_dev, diag_dev]
    partners += [(me_f, me_d, lax.rem(me_r + step, row_shards)) for step in range(1, row_shards)]
    partners += [(me_f, lax.rem(me_d + step, depths), me_r) for step in range(1, depths)]
    barrier = pltpu.get_barrier_semaphore()
    for device in partners:
        pl.semaphore_signal(barrier, inc=1, device_id=device, device_id_type=pl.DeviceIdType.MESH)
    pl.semaphore_wait(barrier, len(partners))

    def slot(frame, row):
        return vol.at[frame, pl.ds(row * rows_here, rows_here)]

    def gather(index, src, frame, row, device):
        return remote(src, slot(frame, row), g_send.at[index], g_recv.at[index], device)

    own_x = gather(0, vin, me_f, me_r, x_dev)
    own_far = gather(1, vin, me_f, me_r, far_dev)
    own_diag = gather(2, vin, me_f, me_r, diag_dev)
    own_core = gather(3, vin, me_f, me_r, core_dev)
    for copy in (own_x, own_far, own_diag, own_core):
        copy.start()
    slot(me_f, me_r)[...] = vin[...]

    w_copy.wait()
    for tap_col in range(TAP_SIDE):
        pieces = [wraw[(TAP_SIDE - 1 - at) * TAP_SIDE + tap_col] for at in range(TAP_SIDE)]
        wflat[tap_col * stride:tap_col * stride + width, :] = jnp.concatenate(pieces, axis=1)
    edge = jnp.zeros((reach * depth_rows, frames * cols), jnp.bfloat16)
    xmask[:reach * depth_rows, :] = edge
    xmask[(rows + reach) * depth_rows:, :] = edge

    own_x.wait_recv()
    fwd_x = gather(4, slot(other_f, me_r), other_f, me_r, core_dev)
    fwd_x.start()
    own_far.wait_recv()
    fwd_far = gather(5, slot(me_f, far_r), me_f, far_r, core_dev)
    fwd_far.start()
    own_diag.wait_recv()
    fwd_diag = gather(6, slot(other_f, far_r), other_f, far_r, core_dev)
    fwd_diag.start()
    for copy in (own_core, fwd_x, fwd_far, fwd_diag):
        copy.wait_recv()

    first_block = me_f * blocks_here
    for row in range(rows):
        for block in range(blocks_here):
            keep = (region[row:row + 1, :] == first_block + block).astype(jnp.float32).astype(jnp.bfloat16)
            top = (row + reach) * depth_rows + block * phases
            for frame in range(frames):
                xmask[top:top + phases, frame * cols:(frame + 1) * cols] = vol[frame, row] * keep

    lane = lax.broadcasted_iota(jnp.int32, (qpad, cols), 1)
    x_copies = []
    for quad in range(quads):
        sums = [[None] * frames for _ in range(depths)]
        for at in range(depths):
            row = quad * depths + at
            slab = xmask[row * depth_rows:(row + TAP_SIDE) * depth_rows, :]
            product = jnp.dot(wflat[...], slab, preferred_element_type=jnp.float32)
            for frame in range(frames):
                total = None
                for tap_col in range(TAP_SIDE):
                    shift = tap_col - reach
                    piece = product[tap_col * stride:tap_col * stride + qpad, frame * cols:(frame + 1) * cols]
                    if shift:
                        piece = pltpu.roll(piece, shift % cols, 1)
                        inside = lane >= shift if shift > 0 else lane < cols + shift
                        piece = jnp.where(inside, piece, 0.0)
                    total = piece if total is None else total + piece
                sums[at][frame] = total
        for frame in range(frames):
            for share in range(depths):
                packed = None
                for at in range(depths):
                    shift = (at - share) * col_share % cols
                    moved = pltpu.roll(sums[at][frame], shift, 1) if shift else sums[at][frame]
                    packed = moved if packed is None else jnp.where(lane >= at * col_share, moved, packed)
                part[frame, quad, share] = packed
        copy = remote(part.at[other_f, quad], xrecv.at[quad], x_send.at[quad], x_recv.at[quad], x_dev)
        copy.start()
        x_copies.append(copy)

    z_copies = []
    for quad in range(quads):
        x_copies[quad].wait_recv()
        for share in range(depths):
            zsend[quad, share] = part[me_f, quad, share] + xrecv[quad, share]
        for step in range(1, depths):
            to = lax.rem(me_d + step, depths)
            copy = remote(zsend.at[quad, to], zrecv.at[quad, step - 1], z_send.at[quad, step - 1],
                          z_recv.at[quad, step - 1], (me_f, to, me_r))
            copy.start()
            z_copies.append(copy)
    for quad in range(quads):
        total = zsend[quad, me_d]
        for step in range(1, depths):
            z_copies[quad * (depths - 1) + step - 1].wait_recv()
            total = total + zrecv[quad, step - 1]
        yred[quad] = total

    shares = row_shards // quads
    y_copies = []
    for step in range(1, row_shards):
        to = lax.rem(me_r + step, row_shards)
        copy = remote(yred.at[to // shares], fin.at[me_r], y_send.at[step - 1], y_recv.at[step - 1], (me_f, me_d, to))
        copy.start()
        y_copies.append(copy)
    fin[me_r] = yred[me_r // shares]
    for copy in y_copies:
        copy.wait_recv()
    lanes_here = rows_here * col_share
    back = lax.rem(cols - lax.rem(me_r, shares) * lanes_here, cols)
    for source in range(row_shards):
        mine = pltpu.roll(fin[source], back, 1)
        cam[:, source * width:(source + 1) * width] = mine.T[:lanes_here, :width]
    for copy in (own_x, own_far, own_diag, own_core, fwd_x, fwd_far, fwd_diag, *x_copies, *z_copies, *y_copies):
        copy.wait_send()


def fused_body(sizes, volume, point_spread, region_map, measured, pixel_weight):
    frames, depths, row_shards = sizes
    _, _, rows_here, merged = volume.shape
    cols = merged // PHASES
    _, depth_rows, taps, width = point_spread.shape
    rows = rows_here * row_shards
    quads = rows // depths
    qpad = round_up(width, 8)
    stride = round_up(width, 16)
    vin = volume.reshape(rows_here, cols, PHASES).transpose(0, 2, 1)
    spread = point_spread.reshape(depth_rows, taps, width).transpose(1, 2, 0)
    col_share = cols // depths
    vmem = pl.BlockSpec(memory_space=pltpu.VMEM)
    dma = pltpu.SemaphoreType.DMA
    cam = pl.pallas_call(
        functools.partial(kernel, frames, depths, row_shards),
        out_shape=jax.ShapeDtypeStruct((rows_here * col_share, row_shards * width), jnp.float32),
        in_specs=[vmem, pl.BlockSpec(memory_space=pl.ANY), vmem],
        out_specs=vmem,
        scratch_shapes=[
            pltpu.VMEM((frames, rows, PHASES, cols), jnp.bfloat16),
            pltpu.VMEM((taps, width, depth_rows), jnp.bfloat16),
            pltpu.VMEM((TAP_SIDE * stride, TAP_SIDE * depth_rows), jnp.bfloat16),
            pltpu.VMEM(((rows + TAP_SIDE - 1) * depth_rows, frames * cols), jnp.bfloat16),
            pltpu.VMEM((frames, quads, depths, qpad, cols), jnp.float32),
            pltpu.VMEM((quads, depths, qpad, cols), jnp.float32),
            pltpu.VMEM((quads, depths, qpad, cols), jnp.float32),
            pltpu.VMEM((quads, depths - 1, qpad, cols), jnp.float32),
            pltpu.VMEM((quads, qpad, cols), jnp.float32),
            pltpu.VMEM((row_shards, qpad, cols), jnp.float32),
            dma, dma((7,)), dma((7,)), dma((quads,)), dma((quads,)),
            dma((quads, depths - 1)), dma((quads, depths - 1)),
            dma((row_shards - 1,)), dma((row_shards - 1,)),
        ],
        compiler_params=pltpu.CompilerParams(collective_id=0, has_side_effects=True),
    )(vin, spread, region_map)
    camera = cam.reshape(measured.shape)
    residual = pixel_weight.astype(jnp.float32) * (camera - measured.astype(jnp.float32))
    return (camera, residual)


def solution(mesh):
    in_specs = (
        P("depth", "frame", "row", None),
        P("depth", "frame", None, "row"),
        P(),
        P("frame", "row", "depth"),
        P("frame", "row", "depth"),
    )
    out_specs = (P("frame", "row", "depth"), P("frame", "row", "depth"))
    sizes = (mesh.shape["frame"], mesh.shape["depth"], mesh.shape["row"])

    def body(volume, *rest):
        rows = volume.shape[2] * sizes[2]
        blocks_fit = rest[0].shape[1] % PHASES == 0
        quads = rows // sizes[1] if rows % sizes[1] == 0 else 0
        packs = quads and sizes[2] % quads == 0 and (volume.shape[3] // PHASES) == 128
        if sizes[0] == 2 and sizes[2] == 4 and volume.shape[1] == 1 and blocks_fit and packs:
            return fused_body(sizes, volume, *rest)
        return plain_body(volume, *rest)

    return jax.shard_map(body, mesh=mesh, in_specs=in_specs, out_specs=out_specs, check_vma=False)
```

```python
import functools
import math

import jax
import jax.numpy as jnp
from jax import lax
from jax.experimental import pallas as pl
from jax.experimental.pallas import tpu as pltpu
from jax.sharding import PartitionSpec as P

PHASES = 144
BLOCKS = 4
TAP_SIDE = 5


def build_taps(planes, region_rows):
    tap_reach = TAP_SIDE // 2
    frames, row_count, merged = planes.shape
    col_count = merged // PHASES
    split_planes = planes.reshape(frames, row_count, col_count, PHASES)
    block_ids = jnp.arange(BLOCKS, dtype=jnp.int32)
    onehot = (region_rows[:, :, None] == block_ids[None, None, :]).astype(jnp.bfloat16)
    expanded = (split_planes[:, :, :, None, :] * onehot[None, :, :, :, None]).reshape(
        frames, row_count, col_count, BLOCKS * PHASES
    )
    return jnp.pad(expanded, ((0, 0), (0, 0), (tap_reach, tap_reach), (0, 0)))


def project(padded, spread_local, out_rows):
    tap_reach = TAP_SIDE // 2
    frames, ext_rows, ext_cols, _ = padded.shape
    col_count = ext_cols - 2 * tap_reach
    out_width = spread_local.shape[2]
    zero_start = jnp.zeros((frames * out_rows * col_count, out_width), jnp.float32)
    running = zero_start
    spread_slab = lax.all_gather(spread_local, "frame", axis=0, tiled=True)
    piece_rows = spread_slab.shape[0]
    flat_cols = padded.reshape(frames * ext_rows * ext_cols, piece_rows)
    for tap_row in range(TAP_SIDE):
        row_taps = spread_slab[:, tap_row * TAP_SIDE : (tap_row + 1) * TAP_SIDE, :].reshape(
            piece_rows, TAP_SIDE * out_width
        )
        product = jnp.dot(flat_cols, row_taps, preferred_element_type=jnp.float32)
        product = product.reshape(frames, ext_rows, ext_cols, TAP_SIDE, out_width)
        first_row = 2 * tap_reach - tap_row
        for tap_col in range(TAP_SIDE):
            first_col = 2 * tap_reach - tap_col
            shifted = product[
                :, first_row : first_row + out_rows, first_col : first_col + col_count, tap_col, :
            ]
            running = running + shifted.reshape(frames * out_rows * col_count, out_width)
    partial_value = running.reshape(frames, out_rows, col_count * out_width)
    return lax.psum_scatter(partial_value, "depth", scatter_dimension=2, tiled=True)


def plain_body(volume, point_spread, region_map, measured, pixel_weight):
    tap_reach = TAP_SIDE // 2
    planes = volume[0]
    row_count = planes.shape[1]
    region_padded = jnp.pad(region_map, ((tap_reach, tap_reach), (0, 0)), constant_values=-1)
    all_rows = lax.all_gather(planes, "row", axis=1, tiled=True)
    extended = jnp.pad(all_rows, ((0, 0), (tap_reach, tap_reach), (0, 0)))
    padded = build_taps(extended, region_padded)
    piece_width = point_spread.shape[3]
    partial_value = project(padded, point_spread[0], all_rows.shape[1])
    frames, total_rows, merged = partial_value.shape
    split_partial = partial_value.reshape(frames, total_rows, merged // piece_width, piece_width)
    returned = lax.all_to_all(split_partial, "row", split_axis=1, concat_axis=3, tiled=True)
    camera = returned.reshape(frames, row_count, returned.shape[2] * returned.shape[3])
    residual = pixel_weight.astype(jnp.float32) * (camera - measured.astype(jnp.float32))
    return (camera, residual)


def round_up(value, step):
    return (value + step - 1) // step * step


def remote(src, dst, send_sem, recv_sem, device):
    return pltpu.make_async_remote_copy(
        src_ref=src, dst_ref=dst, send_sem=send_sem, recv_sem=recv_sem,
        device_id=device, device_id_type=pl.DeviceIdType.MESH,
    )


def lanes_from_rows(raw, wide, pieces, vin):
    rows_here, phases, cols = vin.shape
    group = math.lcm(phases, 128) // phases
    span = group * phases
    groups = cols // group
    wide[:, span:] = jnp.zeros((wide.shape[0], wide.shape[1] - span), jnp.float32)
    for at in range(groups):
        strip = raw[:, at * span:(at + 1) * span].astype(jnp.float32)
        for row in range(rows_here):
            wide[row * groups + at:row * groups + at + 1, :span] = strip[row:row + 1]
    for member in range(group):
        for half in range(pieces.shape[0]):
            first = member * phases + half * 128
            pieces[half, pl.ds(member, rows_here * groups, stride=group), :] = wide[:, first:first + 128]
    for row in range(rows_here):
        for half in range(pieces.shape[0]):
            count = min(128, phases - half * 128)
            turned = pieces[half, row * cols:(row + 1) * cols, :].T
            vin[row, half * 128:half * 128 + count, :] = turned[:count].astype(jnp.bfloat16)


def kernel(frames, depths, row_shards, v_hbm, w_hbm, region, m_hbm, p_hbm, cam, res, raw, wide, pieces, vin,
           mraw, praw, in_sem, vol, wraw, wflat, xmask, part, xrecv, zsend,
           zrecv, yred, fin, w_sem, g_send, g_recv, x_send, x_recv, z_send, z_recv, y_send, y_recv):
    reach = TAP_SIDE // 2
    rows_here, phases, cols = vin.shape
    rows = rows_here * row_shards
    taps, width, depth_rows = w_hbm.shape
    blocks_here = depth_rows // phases
    stride = wflat.shape[0] // TAP_SIDE
    qpad = part.shape[3]
    col_share = cols // depths
    quads = rows // depths
    me_f, me_d, me_r = lax.axis_index("frame"), lax.axis_index("depth"), lax.axis_index("row")
    other_f = 1 - me_f
    core_r = me_r + 1 - 2 * lax.rem(me_r, 2)
    far_r = lax.rem(me_r + 2, row_shards)
    far_core_r = far_r + 1 - 2 * lax.rem(far_r, 2)


    x_dev = (other_f, me_d, me_r)
    core_dev = (me_f, me_d, core_r)
    far_dev = (me_f, me_d, far_r)
    diag_dev = (other_f, me_d, far_r)
    partners = [x_dev, diag_dev]
    partners += [(me_f, me_d, lax.rem(me_r + step, row_shards)) for step in range(1, row_shards)]
    partners += [(me_f, lax.rem(me_d + step, depths), me_r) for step in range(1, depths)]
    barrier = pltpu.get_barrier_semaphore()
    for device in partners:
        pl.semaphore_signal(barrier, inc=1, device_id=device, device_id_type=pl.DeviceIdType.MESH)
    v_copy = pltpu.make_async_copy(v_hbm, raw, in_sem.at[0])
    v_copy.start()
    w_copy = pltpu.make_async_copy(w_hbm, wraw, w_sem)
    w_copy.start()
    m_copy = pltpu.make_async_copy(m_hbm, mraw, in_sem.at[1])
    m_copy.start()
    p_copy = pltpu.make_async_copy(p_hbm, praw, in_sem.at[2])
    p_copy.start()
    v_copy.wait()
    lanes_from_rows(raw, wide, pieces, vin)
    pl.semaphore_wait(barrier, len(partners))

    def slot(frame, row):
        return vol.at[frame, pl.ds(row * rows_here, rows_here)]

    def gather(index, src, frame, row, device):
        return remote(src, slot(frame, row), g_send.at[index], g_recv.at[index], device)

    own_x = gather(0, vin, me_f, me_r, x_dev)
    own_far = gather(1, vin, me_f, me_r, far_dev)
    own_diag = gather(2, vin, me_f, me_r, diag_dev)
    own_core = gather(3, vin, me_f, me_r, core_dev)
    for copy in (own_x, own_far, own_diag, own_core):
        copy.start()
    slot(me_f, me_r)[...] = vin[...]

    w_copy.wait()
    for tap_col in range(TAP_SIDE):
        bands = [wraw[(TAP_SIDE - 1 - at) * TAP_SIDE + tap_col] for at in range(TAP_SIDE)]
        wflat[tap_col * stride:tap_col * stride + width, :] = jnp.concatenate(bands, axis=1)
    edge = jnp.zeros((reach * depth_rows, frames * cols), jnp.bfloat16)
    xmask[:reach * depth_rows, :] = edge
    xmask[(rows + reach) * depth_rows:, :] = edge

    own_x.wait_recv()
    fwd_x = gather(4, slot(other_f, me_r), other_f, me_r, core_dev)
    fwd_x.start()
    own_far.wait_recv()
    fwd_far = gather(5, slot(me_f, far_r), me_f, far_r, core_dev)
    fwd_far.start()
    own_diag.wait_recv()
    fwd_diag = gather(6, slot(other_f, far_r), other_f, far_r, core_dev)
    fwd_diag.start()
    for copy in (own_core, fwd_x, fwd_far, fwd_diag):
        copy.wait_recv()

    first_block = me_f * blocks_here
    for row in range(rows):
        for block in range(blocks_here):
            keep = (region[row:row + 1, :] == first_block + block).astype(jnp.float32).astype(jnp.bfloat16)
            top = (row + reach) * depth_rows + block * phases
            for frame in range(frames):
                xmask[top:top + phases, frame * cols:(frame + 1) * cols] = vol[frame, row] * keep

    lane = lax.broadcasted_iota(jnp.int32, (qpad, cols), 1)
    x_copies = []
    for quad in range(quads):
        sums = [[None] * frames for _ in range(depths)]
        for at in range(depths):
            row = quad * depths + at
            slab = xmask[row * depth_rows:(row + TAP_SIDE) * depth_rows, :]
            product = jnp.dot(wflat[...], slab, preferred_element_type=jnp.float32)
            for frame in range(frames):
                total = None
                for tap_col in range(TAP_SIDE):
                    shift = tap_col - reach
                    piece = product[tap_col * stride:tap_col * stride + qpad, frame * cols:(frame + 1) * cols]
                    if shift:
                        piece = pltpu.roll(piece, shift % cols, 1)
                        inside = lane >= shift if shift > 0 else lane < cols + shift
                        piece = jnp.where(inside, piece, 0.0)
                    total = piece if total is None else total + piece
                sums[at][frame] = total
        for frame in range(frames):
            for share in range(depths):
                packed = None
                for at in range(depths):
                    shift = (at - share) * col_share % cols
                    moved = pltpu.roll(sums[at][frame], shift, 1) if shift else sums[at][frame]
                    packed = moved if packed is None else jnp.where(lane >= at * col_share, moved, packed)
                part[frame, quad, share] = packed
        copy = remote(part.at[other_f, quad], xrecv.at[quad], x_send.at[quad], x_recv.at[quad], x_dev)
        copy.start()
        x_copies.append(copy)

    z_copies = []
    for quad in range(quads):
        x_copies[quad].wait_recv()
        for share in range(depths):
            zsend[quad, share] = part[me_f, quad, share] + xrecv[quad, share]
        for step in range(1, depths):
            to = lax.rem(me_d + step, depths)
            copy = remote(zsend.at[quad, to], zrecv.at[quad, step - 1], z_send.at[quad, step - 1],
                          z_recv.at[quad, step - 1], (me_f, to, me_r))
            copy.start()
            z_copies.append(copy)
    for quad in range(quads):
        total = zsend[quad, me_d]
        for step in range(1, depths):
            z_copies[quad * (depths - 1) + step - 1].wait_recv()
            total = total + zrecv[quad, step - 1]
        yred[quad] = total

    shares = row_shards // quads
    y_copies = []
    for step in range(1, row_shards):
        to = lax.rem(me_r + step, row_shards)
        copy = remote(yred.at[to // shares], fin.at[me_r], y_send.at[step - 1], y_recv.at[step - 1], (me_f, me_d, to))
        copy.start()
        y_copies.append(copy)
    fin[me_r] = yred[me_r // shares]
    for copy in y_copies:
        copy.wait_recv()
    lanes_here = rows_here * col_share
    back = lax.rem(cols - lax.rem(me_r, shares) * lanes_here, cols)
    turned = jnp.concatenate(
        [pltpu.roll(fin[source], back, 1).T[:lanes_here, :width] for source in range(row_shards)], axis=1
    )
    halves = pieces.shape[0]
    for half in range(halves):
        count = min(128, phases - half * 128)
        pieces[half, :lanes_here, :count] = turned[:, half * 128:half * 128 + count]
    group = math.lcm(phases, 128) // phases
    span = group * phases
    per_row = col_share // group
    members = []
    for member in range(group):
        for half in range(halves):
            count = min(128, phases - half * 128)
            members.append(pieces[half, pl.ds(member, rows_here * per_row, stride=group), :][:, :count])
    strips = jnp.concatenate(members, axis=1)
    for row in range(rows_here):
        for at in range(per_row):
            line = row * per_row + at
            cam[row:row + 1, at * span:(at + 1) * span] = strips[line:line + 1]
    m_copy.wait()
    p_copy.wait()
    res[...] = praw[...].astype(jnp.float32) * (cam[...] - mraw[...].astype(jnp.float32))
    for copy in (own_x, own_far, own_diag, own_core, fwd_x, fwd_far, fwd_diag, *x_copies, *z_copies, *y_copies):
        copy.wait_send()


def fused_body(sizes, volume, point_spread, region_map, measured, pixel_weight):
    frames, depths, row_shards = sizes
    _, _, rows_here, merged = volume.shape
    cols = merged // PHASES
    _, depth_rows, taps, width = point_spread.shape
    rows = rows_here * row_shards
    quads = rows // depths
    qpad = round_up(width, 8)
    stride = round_up(width, 16)
    group = math.lcm(PHASES, 128) // PHASES
    span = group * PHASES
    image = (rows_here, cols // depths * PHASES)
    spread = point_spread.reshape(depth_rows, taps, width).transpose(1, 2, 0)
    vmem = pl.BlockSpec(memory_space=pltpu.VMEM)
    hbm = pl.BlockSpec(memory_space=pl.ANY)
    dma = pltpu.SemaphoreType.DMA
    camera, residual = pl.pallas_call(
        functools.partial(kernel, frames, depths, row_shards),
        out_shape=[jax.ShapeDtypeStruct(image, jnp.float32)] * 2,
        in_specs=[hbm, hbm, vmem, hbm, hbm],
        out_specs=[vmem, vmem],
        scratch_shapes=[
            pltpu.VMEM((rows_here, merged), jnp.bfloat16),
            pltpu.VMEM((rows_here * cols // group, span + 128), jnp.float32),
            pltpu.VMEM((round_up(PHASES, 128) // 128, rows_here * cols, 128), jnp.float32),
            pltpu.VMEM((rows_here, PHASES, cols), jnp.bfloat16),
            pltpu.VMEM(image, jnp.bfloat16),
            pltpu.VMEM(image, jnp.int32),
            dma((3,)),
            pltpu.VMEM((frames, rows, PHASES, cols), jnp.bfloat16),
            pltpu.VMEM((taps, width, depth_rows), jnp.bfloat16),
            pltpu.VMEM((TAP_SIDE * stride, TAP_SIDE * depth_rows), jnp.bfloat16),
            pltpu.VMEM(((rows + TAP_SIDE - 1) * depth_rows, frames * cols), jnp.bfloat16),
            pltpu.VMEM((frames, quads, depths, qpad, cols), jnp.float32),
            pltpu.VMEM((quads, depths, qpad, cols), jnp.float32),
            pltpu.VMEM((quads, depths, qpad, cols), jnp.float32),
            pltpu.VMEM((quads, depths - 1, qpad, cols), jnp.float32),
            pltpu.VMEM((quads, qpad, cols), jnp.float32),
            pltpu.VMEM((row_shards, qpad, cols), jnp.float32),
            dma, dma((7,)), dma((7,)), dma((quads,)), dma((quads,)),
            dma((quads, depths - 1)), dma((quads, depths - 1)),
            dma((row_shards - 1,)), dma((row_shards - 1,)),
        ],
        compiler_params=pltpu.CompilerParams(collective_id=0, has_side_effects=True),
    )(volume.reshape(rows_here, merged), spread, region_map, measured.reshape(image), pixel_weight.reshape(image))
    return (camera.reshape(measured.shape), residual.reshape(measured.shape))


def solution(mesh):
    in_specs = (
        P("depth", "frame", "row", None),
        P("depth", "frame", None, "row"),
        P(),
        P("frame", "row", "depth"),
        P("frame", "row", "depth"),
    )
    out_specs = (P("frame", "row", "depth"), P("frame", "row", "depth"))
    sizes = (mesh.shape["frame"], mesh.shape["depth"], mesh.shape["row"])

    def body(volume, *rest):
        rows = volume.shape[2] * sizes[2]
        blocks_fit = rest[0].shape[1] % PHASES == 0
        quads = rows // sizes[1] if rows % sizes[1] == 0 else 0
        packs = quads and sizes[2] % quads == 0 and (volume.shape[3] // PHASES) == 128
        if sizes[0] == 2 and sizes[2] == 4 and volume.shape[1] == 1 and blocks_fit and packs:
            return fused_body(sizes, volume, *rest)
        return plain_body(volume, *rest)

    return jax.shard_map(body, mesh=mesh, in_specs=in_specs, out_specs=out_specs, check_vma=False)
```

```python
import functools
import math

import jax
import jax.numpy as jnp
from jax import lax
from jax.experimental import pallas as pl
from jax.experimental.pallas import tpu as pltpu
from jax.sharding import PartitionSpec as P

PHASES = 144
BLOCKS = 4
TAP_SIDE = 5


def build_taps(planes, region_rows):
    tap_reach = TAP_SIDE // 2
    frames, row_count, merged = planes.shape
    col_count = merged // PHASES
    split_planes = planes.reshape(frames, row_count, col_count, PHASES)
    block_ids = jnp.arange(BLOCKS, dtype=jnp.int32)
    onehot = (region_rows[:, :, None] == block_ids[None, None, :]).astype(jnp.bfloat16)
    expanded = (split_planes[:, :, :, None, :] * onehot[None, :, :, :, None]).reshape(
        frames, row_count, col_count, BLOCKS * PHASES
    )
    return jnp.pad(expanded, ((0, 0), (0, 0), (tap_reach, tap_reach), (0, 0)))


def project(padded, spread_local, out_rows):
    tap_reach = TAP_SIDE // 2
    frames, ext_rows, ext_cols, _ = padded.shape
    col_count = ext_cols - 2 * tap_reach
    out_width = spread_local.shape[2]
    zero_start = jnp.zeros((frames * out_rows * col_count, out_width), jnp.float32)
    running = zero_start
    spread_slab = lax.all_gather(spread_local, "frame", axis=0, tiled=True)
    piece_rows = spread_slab.shape[0]
    flat_cols = padded.reshape(frames * ext_rows * ext_cols, piece_rows)
    for tap_row in range(TAP_SIDE):
        row_taps = spread_slab[:, tap_row * TAP_SIDE : (tap_row + 1) * TAP_SIDE, :].reshape(
            piece_rows, TAP_SIDE * out_width
        )
        product = jnp.dot(flat_cols, row_taps, preferred_element_type=jnp.float32)
        product = product.reshape(frames, ext_rows, ext_cols, TAP_SIDE, out_width)
        first_row = 2 * tap_reach - tap_row
        for tap_col in range(TAP_SIDE):
            first_col = 2 * tap_reach - tap_col
            shifted = product[
                :, first_row : first_row + out_rows, first_col : first_col + col_count, tap_col, :
            ]
            running = running + shifted.reshape(frames * out_rows * col_count, out_width)
    partial_value = running.reshape(frames, out_rows, col_count * out_width)
    return lax.psum_scatter(partial_value, "depth", scatter_dimension=2, tiled=True)


def plain_body(volume, point_spread, region_map, measured, pixel_weight):
    tap_reach = TAP_SIDE // 2
    planes = volume[0]
    row_count = planes.shape[1]
    region_padded = jnp.pad(region_map, ((tap_reach, tap_reach), (0, 0)), constant_values=-1)
    all_rows = lax.all_gather(planes, "row", axis=1, tiled=True)
    extended = jnp.pad(all_rows, ((0, 0), (tap_reach, tap_reach), (0, 0)))
    padded = build_taps(extended, region_padded)
    piece_width = point_spread.shape[3]
    partial_value = project(padded, point_spread[0], all_rows.shape[1])
    frames, total_rows, merged = partial_value.shape
    split_partial = partial_value.reshape(frames, total_rows, merged // piece_width, piece_width)
    returned = lax.all_to_all(split_partial, "row", split_axis=1, concat_axis=3, tiled=True)
    camera = returned.reshape(frames, row_count, returned.shape[2] * returned.shape[3])
    residual = pixel_weight.astype(jnp.float32) * (camera - measured.astype(jnp.float32))
    return (camera, residual)


def round_up(value, step):
    return (value + step - 1) // step * step


def remote(src, dst, send_sem, recv_sem, device):
    return pltpu.make_async_remote_copy(
        src_ref=src, dst_ref=dst, send_sem=send_sem, recv_sem=recv_sem,
        device_id=device, device_id_type=pl.DeviceIdType.MESH,
    )


def lanes_from_rows(raw, wide, pieces, vin):
    rows_here, phases, cols = vin.shape
    group = math.lcm(phases, 128) // phases
    span = group * phases
    groups = cols // group
    wide[:, span:] = jnp.zeros((wide.shape[0], wide.shape[1] - span), jnp.float32)
    for at in range(groups):
        strip = raw[:, at * span:(at + 1) * span].astype(jnp.float32)
        for row in range(rows_here):
            wide[row * groups + at:row * groups + at + 1, :span] = strip[row:row + 1]
    for member in range(group):
        for half in range(pieces.shape[0]):
            first = member * phases + half * 128
            pieces[half, pl.ds(member, rows_here * groups, stride=group), :] = wide[:, first:first + 128]
    for row in range(rows_here):
        for half in range(pieces.shape[0]):
            count = min(128, phases - half * 128)
            turned = pieces[half, row * cols:(row + 1) * cols, :].T
            vin[row, half * 128:half * 128 + count, :] = turned[:count].astype(jnp.bfloat16)


def kernel(frames, depths, row_shards, v_hbm, w_hbm, region, m_hbm, p_hbm, cam, res, raw, wide, pieces, vin,
           mraw, praw, in_sem, vol, wraw, wflat, xmask, part, xrecv, zsend,
           zrecv, yred, fin, w_sem, g_send, g_recv, x_send, x_recv, z_send, z_recv, y_send, y_recv):
    reach = TAP_SIDE // 2
    rows_here, phases, cols = vin.shape
    rows = rows_here * row_shards
    taps, width, depth_rows = w_hbm.shape
    blocks_here = depth_rows // phases
    stride = wflat.shape[0] // TAP_SIDE
    qpad = part.shape[3]
    col_share = cols // depths
    quads = rows // depths
    me_f, me_d, me_r = lax.axis_index("frame"), lax.axis_index("depth"), lax.axis_index("row")
    other_f = 1 - me_f
    core_r = me_r + 1 - 2 * lax.rem(me_r, 2)
    far_r = lax.rem(me_r + 2, row_shards)
    far_core_r = far_r + 1 - 2 * lax.rem(far_r, 2)


    x_dev = (other_f, me_d, me_r)
    core_dev = (me_f, me_d, core_r)
    far_dev = (me_f, me_d, far_r)
    diag_dev = (other_f, me_d, far_r)
    partners = [x_dev, diag_dev]
    partners += [(me_f, me_d, lax.rem(me_r + step, row_shards)) for step in range(1, row_shards)]
    partners += [(me_f, lax.rem(me_d + step, depths), me_r) for step in range(1, depths)]
    barrier = pltpu.get_barrier_semaphore()
    for device in partners:
        pl.semaphore_signal(barrier, inc=1, device_id=device, device_id_type=pl.DeviceIdType.MESH)
    v_copy = pltpu.make_async_copy(v_hbm, raw, in_sem.at[0])
    v_copy.start()
    w_copy = pltpu.make_async_copy(w_hbm, wraw, w_sem)
    w_copy.start()
    m_copy = pltpu.make_async_copy(m_hbm, mraw, in_sem.at[1])
    m_copy.start()
    p_copy = pltpu.make_async_copy(p_hbm, praw, in_sem.at[2])
    p_copy.start()
    v_copy.wait()
    lanes_from_rows(raw, wide, pieces, vin)
    pl.semaphore_wait(barrier, len(partners))

    def slot(frame, row):
        return vol.at[frame, pl.ds(row * rows_here, rows_here)]

    def gather(index, src, frame, row, device):
        return remote(src, slot(frame, row), g_send.at[index], g_recv.at[index], device)

    own_x = gather(0, vin, me_f, me_r, x_dev)
    own_far = gather(1, vin, me_f, me_r, far_dev)
    own_diag = gather(2, vin, me_f, me_r, diag_dev)
    own_core = gather(3, vin, me_f, me_r, core_dev)
    for copy in (own_x, own_far, own_diag, own_core):
        copy.start()
    slot(me_f, me_r)[...] = vin[...]

    w_copy.wait()
    for tap_col in range(TAP_SIDE):
        bands = [wraw[(TAP_SIDE - 1 - at) * TAP_SIDE + tap_col] for at in range(TAP_SIDE)]
        wflat[tap_col * stride:tap_col * stride + width, :] = jnp.concatenate(bands, axis=1)
    edge = jnp.zeros((reach * depth_rows, frames * cols), jnp.bfloat16)
    xmask[:reach * depth_rows, :] = edge
    xmask[(rows + reach) * depth_rows:, :] = edge

    own_x.wait_recv()
    fwd_x = gather(4, slot(other_f, me_r), other_f, me_r, core_dev)
    fwd_x.start()
    own_far.wait_recv()
    fwd_far = gather(5, slot(me_f, far_r), me_f, far_r, core_dev)
    fwd_far.start()
    own_diag.wait_recv()
    fwd_diag = gather(6, slot(other_f, far_r), other_f, far_r, core_dev)
    fwd_diag.start()
    for copy in (own_core, fwd_x, fwd_far, fwd_diag):
        copy.wait_recv()

    first_block = me_f * blocks_here
    for row in range(rows):
        for block in range(blocks_here):
            keep = (region[row:row + 1, :] == first_block + block).astype(jnp.float32).astype(jnp.bfloat16)
            top = (row + reach) * depth_rows + block * phases
            for frame in range(frames):
                xmask[top:top + phases, frame * cols:(frame + 1) * cols] = vol[frame, row] * keep

    lane = lax.broadcasted_iota(jnp.int32, (qpad, cols), 1)
    order = sorted(range(1, depths), key=lambda step: abs(step - depths // 2))
    x_copies, z_copies = {}, {}

    def frame_copy(quad, step):
        share = lax.rem(me_d + step, depths)
        return remote(part.at[other_f, quad, share], xrecv.at[quad, share], x_send.at[quad, step],
                      x_recv.at[quad, step], x_dev)

    for quad in range(quads):
        sums = [[None] * frames for _ in range(depths)]
        for at in range(depths):
            row = quad * depths + at
            slab = xmask[row * depth_rows:(row + TAP_SIDE) * depth_rows, :]
            product = jnp.dot(wflat[...], slab, preferred_element_type=jnp.float32)
            for frame in range(frames):
                total = None
                for tap_col in range(TAP_SIDE):
                    shift = tap_col - reach
                    piece = product[tap_col * stride:tap_col * stride + qpad, frame * cols:(frame + 1) * cols]
                    if shift:
                        piece = pltpu.roll(piece, shift % cols, 1)
                        inside = lane >= shift if shift > 0 else lane < cols + shift
                        piece = jnp.where(inside, piece, 0.0)
                    total = piece if total is None else total + piece
                sums[at][frame] = total
        for frame in range(frames):
            for share in range(depths):
                packed = None
                for at in range(depths):
                    shift = (at - share) * col_share % cols
                    moved = pltpu.roll(sums[at][frame], shift, 1) if shift else sums[at][frame]
                    packed = moved if packed is None else jnp.where(lane >= at * col_share, moved, packed)
                part[frame, quad, share] = packed
        for step in order:
            x_copies[quad, step] = frame_copy(quad, step)
            x_copies[quad, step].start()

    for quad in range(quads):
        x_copies[quad, 0] = frame_copy(quad, 0)
        x_copies[quad, 0].start()
    for quad in range(quads):
        for step in order:
            to = lax.rem(me_d + step, depths)
            x_copies[quad, step].wait_recv()
            zsend[quad, to] = part[me_f, quad, to] + xrecv[quad, to]
            z_copies[quad, step] = remote(zsend.at[quad, to], zrecv.at[quad, step - 1], z_send.at[quad, step - 1],
                                          z_recv.at[quad, step - 1], (me_f, to, me_r))
            z_copies[quad, step].start()
    for quad in range(quads):
        x_copies[quad, 0].wait_recv()
        total = part[me_f, quad, me_d] + xrecv[quad, me_d]
        for step in order:
            z_copies[quad, step].wait_recv()
            total = total + zrecv[quad, step - 1]
        yred[quad] = total

    shares = row_shards // quads
    y_copies = []
    for step in range(1, row_shards):
        to = lax.rem(me_r + step, row_shards)
        copy = remote(yred.at[to // shares], fin.at[me_r], y_send.at[step - 1], y_recv.at[step - 1], (me_f, me_d, to))
        copy.start()
        y_copies.append(copy)
    fin[me_r] = yred[me_r // shares]
    for copy in y_copies:
        copy.wait_recv()
    lanes_here = rows_here * col_share
    back = lax.rem(cols - lax.rem(me_r, shares) * lanes_here, cols)
    turned = jnp.concatenate(
        [pltpu.roll(fin[source], back, 1).T[:lanes_here, :width] for source in range(row_shards)], axis=1
    )
    halves = pieces.shape[0]
    for half in range(halves):
        count = min(128, phases - half * 128)
        pieces[half, :lanes_here, :count] = turned[:, half * 128:half * 128 + count]
    group = math.lcm(phases, 128) // phases
    span = group * phases
    per_row = col_share // group
    members = []
    for member in range(group):
        for half in range(halves):
            count = min(128, phases - half * 128)
            members.append(pieces[half, pl.ds(member, rows_here * per_row, stride=group), :][:, :count])
    strips = jnp.concatenate(members, axis=1)
    for row in range(rows_here):
        for at in range(per_row):
            line = row * per_row + at
            cam[row:row + 1, at * span:(at + 1) * span] = strips[line:line + 1]
    m_copy.wait()
    p_copy.wait()
    res[...] = praw[...].astype(jnp.float32) * (cam[...] - mraw[...].astype(jnp.float32))
    for copy in (own_x, own_far, own_diag, own_core, fwd_x, fwd_far, fwd_diag, *x_copies.values(), *z_copies.values(), *y_copies):
        copy.wait_send()


def fused_body(sizes, volume, point_spread, region_map, measured, pixel_weight):
    frames, depths, row_shards = sizes
    _, _, rows_here, merged = volume.shape
    cols = merged // PHASES
    _, depth_rows, taps, width = point_spread.shape
    rows = rows_here * row_shards
    quads = rows // depths
    qpad = width
    stride = round_up(width, 16)
    group = math.lcm(PHASES, 128) // PHASES
    span = group * PHASES
    image = (rows_here, cols // depths * PHASES)
    spread = point_spread.reshape(depth_rows, taps, width).transpose(1, 2, 0)
    vmem = pl.BlockSpec(memory_space=pltpu.VMEM)
    hbm = pl.BlockSpec(memory_space=pl.ANY)
    dma = pltpu.SemaphoreType.DMA
    camera, residual = pl.pallas_call(
        functools.partial(kernel, frames, depths, row_shards),
        out_shape=[jax.ShapeDtypeStruct(image, jnp.float32)] * 2,
        in_specs=[hbm, hbm, vmem, hbm, hbm],
        out_specs=[vmem, vmem],
        scratch_shapes=[
            pltpu.VMEM((rows_here, merged), jnp.bfloat16),
            pltpu.VMEM((rows_here * cols // group, span + 128), jnp.float32),
            pltpu.VMEM((round_up(PHASES, 128) // 128, rows_here * cols, 128), jnp.float32),
            pltpu.VMEM((rows_here, PHASES, cols), jnp.bfloat16),
            pltpu.VMEM(image, jnp.bfloat16),
            pltpu.VMEM(image, jnp.int32),
            dma((3,)),
            pltpu.VMEM((frames, rows, PHASES, cols), jnp.bfloat16),
            pltpu.VMEM((taps, width, depth_rows), jnp.bfloat16),
            pltpu.VMEM((TAP_SIDE * stride, TAP_SIDE * depth_rows), jnp.bfloat16),
            pltpu.VMEM(((rows + TAP_SIDE - 1) * depth_rows, frames * cols), jnp.bfloat16),
            pltpu.VMEM((frames, quads, depths, qpad, cols), jnp.float32),
            pltpu.VMEM((quads, depths, qpad, cols), jnp.float32),
            pltpu.VMEM((quads, depths, qpad, cols), jnp.float32),
            pltpu.VMEM((quads, depths - 1, qpad, cols), jnp.float32),
            pltpu.VMEM((quads, qpad, cols), jnp.float32),
            pltpu.VMEM((row_shards, qpad, cols), jnp.float32),
            dma, dma((7,)), dma((7,)), dma((quads, depths)), dma((quads, depths)),
            dma((quads, depths - 1)), dma((quads, depths - 1)),
            dma((row_shards - 1,)), dma((row_shards - 1,)),
        ],
        compiler_params=pltpu.CompilerParams(collective_id=0, has_side_effects=True),
    )(volume.reshape(rows_here, merged), spread, region_map, measured.reshape(image), pixel_weight.reshape(image))
    return (camera.reshape(measured.shape), residual.reshape(measured.shape))


def solution(mesh):
    in_specs = (
        P("depth", "frame", "row", None),
        P("depth", "frame", None, "row"),
        P(),
        P("frame", "row", "depth"),
        P("frame", "row", "depth"),
    )
    out_specs = (P("frame", "row", "depth"), P("frame", "row", "depth"))
    sizes = (mesh.shape["frame"], mesh.shape["depth"], mesh.shape["row"])

    def body(volume, *rest):
        rows = volume.shape[2] * sizes[2]
        blocks_fit = rest[0].shape[1] % PHASES == 0
        quads = rows // sizes[1] if rows % sizes[1] == 0 else 0
        packs = quads and sizes[2] % quads == 0 and (volume.shape[3] // PHASES) == 128
        if sizes[0] == 2 and sizes[2] == 4 and volume.shape[1] == 1 and blocks_fit and packs:
            return fused_body(sizes, volume, *rest)
        return plain_body(volume, *rest)

    return jax.shard_map(body, mesh=mesh, in_specs=in_specs, out_specs=out_specs, check_vma=False)
```

```python
import functools
import math

import jax
import jax.numpy as jnp
from jax import lax
from jax.experimental import pallas as pl
from jax.experimental.pallas import tpu as pltpu
from jax.sharding import PartitionSpec as P

PHASES = 144
BLOCKS = 4
TAP_SIDE = 5


def build_taps(planes, region_rows):
    tap_reach = TAP_SIDE // 2
    frames, row_count, merged = planes.shape
    col_count = merged // PHASES
    split_planes = planes.reshape(frames, row_count, col_count, PHASES)
    block_ids = jnp.arange(BLOCKS, dtype=jnp.int32)
    onehot = (region_rows[:, :, None] == block_ids[None, None, :]).astype(jnp.bfloat16)
    expanded = (split_planes[:, :, :, None, :] * onehot[None, :, :, :, None]).reshape(
        frames, row_count, col_count, BLOCKS * PHASES
    )
    return jnp.pad(expanded, ((0, 0), (0, 0), (tap_reach, tap_reach), (0, 0)))


def project(padded, spread_local, out_rows):
    tap_reach = TAP_SIDE // 2
    frames, ext_rows, ext_cols, _ = padded.shape
    col_count = ext_cols - 2 * tap_reach
    out_width = spread_local.shape[2]
    zero_start = jnp.zeros((frames * out_rows * col_count, out_width), jnp.float32)
    running = zero_start
    spread_slab = lax.all_gather(spread_local, "frame", axis=0, tiled=True)
    piece_rows = spread_slab.shape[0]
    flat_cols = padded.reshape(frames * ext_rows * ext_cols, piece_rows)
    for tap_row in range(TAP_SIDE):
        row_taps = spread_slab[:, tap_row * TAP_SIDE : (tap_row + 1) * TAP_SIDE, :].reshape(
            piece_rows, TAP_SIDE * out_width
        )
        product = jnp.dot(flat_cols, row_taps, preferred_element_type=jnp.float32)
        product = product.reshape(frames, ext_rows, ext_cols, TAP_SIDE, out_width)
        first_row = 2 * tap_reach - tap_row
        for tap_col in range(TAP_SIDE):
            first_col = 2 * tap_reach - tap_col
            shifted = product[
                :, first_row : first_row + out_rows, first_col : first_col + col_count, tap_col, :
            ]
            running = running + shifted.reshape(frames * out_rows * col_count, out_width)
    partial_value = running.reshape(frames, out_rows, col_count * out_width)
    return lax.psum_scatter(partial_value, "depth", scatter_dimension=2, tiled=True)


def plain_body(volume, point_spread, region_map, measured, pixel_weight):
    tap_reach = TAP_SIDE // 2
    planes = volume[0]
    row_count = planes.shape[1]
    region_padded = jnp.pad(region_map, ((tap_reach, tap_reach), (0, 0)), constant_values=-1)
    all_rows = lax.all_gather(planes, "row", axis=1, tiled=True)
    extended = jnp.pad(all_rows, ((0, 0), (tap_reach, tap_reach), (0, 0)))
    padded = build_taps(extended, region_padded)
    piece_width = point_spread.shape[3]
    partial_value = project(padded, point_spread[0], all_rows.shape[1])
    frames, total_rows, merged = partial_value.shape
    split_partial = partial_value.reshape(frames, total_rows, merged // piece_width, piece_width)
    returned = lax.all_to_all(split_partial, "row", split_axis=1, concat_axis=3, tiled=True)
    camera = returned.reshape(frames, row_count, returned.shape[2] * returned.shape[3])
    residual = pixel_weight.astype(jnp.float32) * (camera - measured.astype(jnp.float32))
    return (camera, residual)


def round_up(value, step):
    return (value + step - 1) // step * step


def remote(src, dst, send_sem, recv_sem, device):
    return pltpu.make_async_remote_copy(
        src_ref=src, dst_ref=dst, send_sem=send_sem, recv_sem=recv_sem,
        device_id=device, device_id_type=pl.DeviceIdType.MESH,
    )


def lanes_from_rows(raw, wide, pieces, vin):
    rows_here, phases, cols = vin.shape
    group = math.lcm(phases, 128) // phases
    span = group * phases
    groups = cols // group
    wide[:, span:] = jnp.zeros((wide.shape[0], wide.shape[1] - span), jnp.float32)
    for at in range(groups):
        strip = raw[:, at * span:(at + 1) * span].astype(jnp.float32)
        for row in range(rows_here):
            wide[row * groups + at:row * groups + at + 1, :span] = strip[row:row + 1]
    for member in range(group):
        for half in range(pieces.shape[0]):
            first = member * phases + half * 128
            pieces[half, pl.ds(member, rows_here * groups, stride=group), :] = wide[:, first:first + 128]
    for row in range(rows_here):
        for half in range(pieces.shape[0]):
            count = min(128, phases - half * 128)
            turned = pieces[half, row * cols:(row + 1) * cols, :].T
            vin[row, half * 128:half * 128 + count, :] = turned[:count].astype(jnp.bfloat16)


def kernel(frames, depths, row_shards, v_hbm, w_hbm, region, m_hbm, p_hbm, cam, res, raw, wide, pieces, vin,
           mraw, praw, in_sem, vol, wraw, wflat, xmask, part, xrecv, zsend,
           zrecv, yred, fin, w_sem, g_send, g_recv, x_send, x_recv, z_send, z_recv, y_send, y_recv):
    reach = TAP_SIDE // 2
    rows_here, phases, cols = vin.shape
    rows = rows_here * row_shards
    taps, width, depth_rows = w_hbm.shape
    blocks_here = depth_rows // phases
    stride = wflat.shape[0] // TAP_SIDE
    qpad = part.shape[3]
    col_share = cols // depths
    quads = rows // depths
    me_f, me_d, me_r = lax.axis_index("frame"), lax.axis_index("depth"), lax.axis_index("row")
    other_f = 1 - me_f
    core_r = me_r + 1 - 2 * lax.rem(me_r, 2)
    far_r = lax.rem(me_r + 2, row_shards)
    far_core_r = far_r + 1 - 2 * lax.rem(far_r, 2)


    x_dev = (other_f, me_d, me_r)
    core_dev = (me_f, me_d, core_r)
    far_dev = (me_f, me_d, far_r)
    diag_dev = (other_f, me_d, far_r)
    partners = [x_dev, diag_dev]
    partners += [(me_f, me_d, lax.rem(me_r + step, row_shards)) for step in range(1, row_shards)]
    partners += [(me_f, lax.rem(me_d + step, depths), me_r) for step in range(1, depths)]
    barrier = pltpu.get_barrier_semaphore()
    for device in partners:
        pl.semaphore_signal(barrier, inc=1, device_id=device, device_id_type=pl.DeviceIdType.MESH)
    v_copy = pltpu.make_async_copy(v_hbm, raw, in_sem.at[0])
    v_copy.start()
    w_copy = pltpu.make_async_copy(w_hbm, wraw, w_sem)
    w_copy.start()
    m_copy = pltpu.make_async_copy(m_hbm, mraw, in_sem.at[1])
    m_copy.start()
    p_copy = pltpu.make_async_copy(p_hbm, praw, in_sem.at[2])
    p_copy.start()
    v_copy.wait()
    lanes_from_rows(raw, wide, pieces, vin)
    pl.semaphore_wait(barrier, len(partners))

    def slot(frame, row):
        return vol.at[frame, pl.ds(row * rows_here, rows_here)]

    def gather(index, src, frame, row, device):
        return remote(src, slot(frame, row), g_send.at[index], g_recv.at[index], device)

    own_x = gather(0, vin, me_f, me_r, x_dev)
    own_far = gather(1, vin, me_f, me_r, far_dev)
    own_diag = gather(2, vin, me_f, me_r, diag_dev)
    own_core = gather(3, vin, me_f, me_r, core_dev)
    for copy in (own_x, own_far, own_diag, own_core):
        copy.start()
    slot(me_f, me_r)[...] = vin[...]

    w_copy.wait()
    for tap_col in range(TAP_SIDE):
        bands = [wraw[(TAP_SIDE - 1 - at) * TAP_SIDE + tap_col] for at in range(TAP_SIDE)]
        wflat[tap_col * stride:tap_col * stride + width, :] = jnp.concatenate(bands, axis=1)
    edge = jnp.zeros((reach * depth_rows, frames * cols), jnp.bfloat16)
    xmask[:reach * depth_rows, :] = edge
    xmask[(rows + reach) * depth_rows:, :] = edge

    own_x.wait_recv()
    fwd_x = gather(4, slot(other_f, me_r), other_f, me_r, core_dev)
    fwd_x.start()
    own_far.wait_recv()
    fwd_far = gather(5, slot(me_f, far_r), me_f, far_r, core_dev)
    fwd_far.start()
    own_diag.wait_recv()
    fwd_diag = gather(6, slot(other_f, far_r), other_f, far_r, core_dev)
    fwd_diag.start()
    for copy in (own_core, fwd_x, fwd_far, fwd_diag):
        copy.wait_recv()

    first_block = me_f * blocks_here
    for row in range(rows):
        for block in range(blocks_here):
            keep = (region[row:row + 1, :] == first_block + block).astype(jnp.float32).astype(jnp.bfloat16)
            top = (row + reach) * depth_rows + block * phases
            for frame in range(frames):
                xmask[top:top + phases, frame * cols:(frame + 1) * cols] = vol[frame, row] * keep

    lane = lax.broadcasted_iota(jnp.int32, (qpad, cols), 1)
    order = sorted(range(1, depths), key=lambda step: abs(step - depths // 2))
    x_copies, z_copies = {}, {}

    def frame_copy(quad, step):
        share = lax.rem(me_d + step, depths)
        return remote(part.at[other_f, quad, share], xrecv.at[quad, share], x_send.at[quad, step],
                      x_recv.at[quad, step], x_dev)

    for quad in range(quads):
        sums = [[None] * frames for _ in range(depths)]
        for at in range(depths):
            row = quad * depths + at
            slab = xmask[row * depth_rows:(row + TAP_SIDE) * depth_rows, :]
            product = jnp.dot(wflat[...], slab, preferred_element_type=jnp.float32)
            for frame in range(frames):
                total = None
                for tap_col in range(TAP_SIDE):
                    shift = tap_col - reach
                    piece = product[tap_col * stride:tap_col * stride + qpad, frame * cols:(frame + 1) * cols]
                    if shift:
                        piece = pltpu.roll(piece, shift % cols, 1)
                        inside = lane >= shift if shift > 0 else lane < cols + shift
                        piece = jnp.where(inside, piece, 0.0)
                    total = piece if total is None else total + piece
                sums[at][frame] = total
        for frame in range(frames):
            for share in range(depths):
                packed = None
                for at in range(depths):
                    shift = (at - share) * col_share % cols
                    moved = pltpu.roll(sums[at][frame], shift, 1) if shift else sums[at][frame]
                    packed = moved if packed is None else jnp.where(lane >= at * col_share, moved, packed)
                part[frame, quad, share] = packed
        for step in order:
            x_copies[quad, step] = frame_copy(quad, step)
            x_copies[quad, step].start()

    for quad in range(quads):
        x_copies[quad, 0] = frame_copy(quad, 0)
        x_copies[quad, 0].start()
    for quad in range(quads):
        for step in order:
            to = lax.rem(me_d + step, depths)
            x_copies[quad, step].wait_recv()
            zsend[quad, to] = part[me_f, quad, to] + xrecv[quad, to]
            z_copies[quad, step] = remote(zsend.at[quad, to], zrecv.at[quad, step - 1], z_send.at[quad, step - 1],
                                          z_recv.at[quad, step - 1], (me_f, to, me_r))
            z_copies[quad, step].start()
    shares = row_shards // quads

    def row_copy(to):
        return remote(yred.at[to // shares], fin.at[me_r], y_send.at[to], y_recv.at[me_r], (me_f, me_d, to))

    for quad in range(quads):
        x_copies[quad, 0].wait_recv()
        total = part[me_f, quad, me_d] + xrecv[quad, me_d]
        for step in order:
            z_copies[quad, step].wait_recv()
            total = total + zrecv[quad, step - 1]
        yred[quad] = total
        for to in range(quad * shares, (quad + 1) * shares):
            @pl.when(to != me_r)
            def _():
                row_copy(to).start()
    fin[me_r] = yred[me_r // shares]
    for source in range(row_shards):
        @pl.when(source != me_r)
        def _():
            remote(yred.at[0], fin.at[source], y_send.at[source], y_recv.at[source],
                   (me_f, me_d, source)).wait_recv()
            row_copy(source).wait_send()
    lanes_here = rows_here * col_share
    back = lax.rem(cols - lax.rem(me_r, shares) * lanes_here, cols)
    turned = jnp.concatenate(
        [pltpu.roll(fin[source], back, 1).T[:lanes_here, :width] for source in range(row_shards)], axis=1
    )
    halves = pieces.shape[0]
    for half in range(halves):
        count = min(128, phases - half * 128)
        pieces[half, :lanes_here, :count] = turned[:, half * 128:half * 128 + count]
    group = math.lcm(phases, 128) // phases
    span = group * phases
    per_row = col_share // group
    members = []
    for member in range(group):
        for half in range(halves):
            count = min(128, phases - half * 128)
            members.append(pieces[half, pl.ds(member, rows_here * per_row, stride=group), :][:, :count])
    strips = jnp.concatenate(members, axis=1)
    for row in range(rows_here):
        for at in range(per_row):
            line = row * per_row + at
            cam[row:row + 1, at * span:(at + 1) * span] = strips[line:line + 1]
    m_copy.wait()
    p_copy.wait()
    res[...] = praw[...].astype(jnp.float32) * (cam[...] - mraw[...].astype(jnp.float32))
    for copy in (own_x, own_far, own_diag, own_core, fwd_x, fwd_far, fwd_diag, *x_copies.values(), *z_copies.values()):
        copy.wait_send()


def fused_body(sizes, volume, point_spread, region_map, measured, pixel_weight):
    frames, depths, row_shards = sizes
    _, _, rows_here, merged = volume.shape
    cols = merged // PHASES
    _, depth_rows, taps, width = point_spread.shape
    rows = rows_here * row_shards
    quads = rows // depths
    qpad = width
    stride = round_up(width, 16)
    group = math.lcm(PHASES, 128) // PHASES
    span = group * PHASES
    image = (rows_here, cols // depths * PHASES)
    spread = point_spread.reshape(depth_rows, taps, width).transpose(1, 2, 0)
    vmem = pl.BlockSpec(memory_space=pltpu.VMEM)
    hbm = pl.BlockSpec(memory_space=pl.ANY)
    dma = pltpu.SemaphoreType.DMA
    camera, residual = pl.pallas_call(
        functools.partial(kernel, frames, depths, row_shards),
        out_shape=[jax.ShapeDtypeStruct(image, jnp.float32)] * 2,
        in_specs=[hbm, hbm, vmem, hbm, hbm],
        out_specs=[vmem, vmem],
        scratch_shapes=[
            pltpu.VMEM((rows_here, merged), jnp.bfloat16),
            pltpu.VMEM((rows_here * cols // group, span + 128), jnp.float32),
            pltpu.VMEM((round_up(PHASES, 128) // 128, rows_here * cols, 128), jnp.float32),
            pltpu.VMEM((rows_here, PHASES, cols), jnp.bfloat16),
            pltpu.VMEM(image, jnp.bfloat16),
            pltpu.VMEM(image, jnp.int32),
            dma((3,)),
            pltpu.VMEM((frames, rows, PHASES, cols), jnp.bfloat16),
            pltpu.VMEM((taps, width, depth_rows), jnp.bfloat16),
            pltpu.VMEM((TAP_SIDE * stride, TAP_SIDE * depth_rows), jnp.bfloat16),
            pltpu.VMEM(((rows + TAP_SIDE - 1) * depth_rows, frames * cols), jnp.bfloat16),
            pltpu.VMEM((frames, quads, depths, qpad, cols), jnp.float32),
            pltpu.VMEM((quads, depths, qpad, cols), jnp.float32),
            pltpu.VMEM((quads, depths, qpad, cols), jnp.float32),
            pltpu.VMEM((quads, depths - 1, qpad, cols), jnp.float32),
            pltpu.VMEM((quads, qpad, cols), jnp.float32),
            pltpu.VMEM((row_shards, qpad, cols), jnp.float32),
            dma, dma((7,)), dma((7,)), dma((quads, depths)), dma((quads, depths)),
            dma((quads, depths - 1)), dma((quads, depths - 1)),
            dma((row_shards,)), dma((row_shards,)),
        ],
        compiler_params=pltpu.CompilerParams(collective_id=0, has_side_effects=True),
    )(volume.reshape(rows_here, merged), spread, region_map, measured.reshape(image), pixel_weight.reshape(image))
    return (camera.reshape(measured.shape), residual.reshape(measured.shape))


def solution(mesh):
    in_specs = (
        P("depth", "frame", "row", None),
        P("depth", "frame", None, "row"),
        P(),
        P("frame", "row", "depth"),
        P("frame", "row", "depth"),
    )
    out_specs = (P("frame", "row", "depth"), P("frame", "row", "depth"))
    sizes = (mesh.shape["frame"], mesh.shape["depth"], mesh.shape["row"])

    def body(volume, *rest):
        rows = volume.shape[2] * sizes[2]
        blocks_fit = rest[0].shape[1] % PHASES == 0
        quads = rows // sizes[1] if rows % sizes[1] == 0 else 0
        packs = quads and sizes[2] % quads == 0 and (volume.shape[3] // PHASES) == 128
        if sizes[0] == 2 and sizes[2] == 4 and volume.shape[1] == 1 and blocks_fit and packs:
            return fused_body(sizes, volume, *rest)
        return plain_body(volume, *rest)

    return jax.shard_map(body, mesh=mesh, in_specs=in_specs, out_specs=out_specs, check_vma=False)
```

```python
import functools
import math

import jax
import jax.numpy as jnp
from jax import lax
from jax.experimental import pallas as pl
from jax.experimental.pallas import tpu as pltpu
from jax.sharding import PartitionSpec as P

PHASES = 144
BLOCKS = 4
TAP_SIDE = 5


def build_taps(planes, region_rows):
    tap_reach = TAP_SIDE // 2
    frames, row_count, merged = planes.shape
    col_count = merged // PHASES
    split_planes = planes.reshape(frames, row_count, col_count, PHASES)
    block_ids = jnp.arange(BLOCKS, dtype=jnp.int32)
    onehot = (region_rows[:, :, None] == block_ids[None, None, :]).astype(jnp.bfloat16)
    expanded = (split_planes[:, :, :, None, :] * onehot[None, :, :, :, None]).reshape(
        frames, row_count, col_count, BLOCKS * PHASES
    )
    return jnp.pad(expanded, ((0, 0), (0, 0), (tap_reach, tap_reach), (0, 0)))


def project(padded, spread_local, out_rows):
    tap_reach = TAP_SIDE // 2
    frames, ext_rows, ext_cols, _ = padded.shape
    col_count = ext_cols - 2 * tap_reach
    out_width = spread_local.shape[2]
    zero_start = jnp.zeros((frames * out_rows * col_count, out_width), jnp.float32)
    running = zero_start
    spread_slab = lax.all_gather(spread_local, "frame", axis=0, tiled=True)
    piece_rows = spread_slab.shape[0]
    flat_cols = padded.reshape(frames * ext_rows * ext_cols, piece_rows)
    for tap_row in range(TAP_SIDE):
        row_taps = spread_slab[:, tap_row * TAP_SIDE : (tap_row + 1) * TAP_SIDE, :].reshape(
            piece_rows, TAP_SIDE * out_width
        )
        product = jnp.dot(flat_cols, row_taps, preferred_element_type=jnp.float32)
        product = product.reshape(frames, ext_rows, ext_cols, TAP_SIDE, out_width)
        first_row = 2 * tap_reach - tap_row
        for tap_col in range(TAP_SIDE):
            first_col = 2 * tap_reach - tap_col
            shifted = product[
                :, first_row : first_row + out_rows, first_col : first_col + col_count, tap_col, :
            ]
            running = running + shifted.reshape(frames * out_rows * col_count, out_width)
    partial_value = running.reshape(frames, out_rows, col_count * out_width)
    return lax.psum_scatter(partial_value, "depth", scatter_dimension=2, tiled=True)


def plain_body(volume, point_spread, region_map, measured, pixel_weight):
    tap_reach = TAP_SIDE // 2
    planes = volume[0]
    row_count = planes.shape[1]
    region_padded = jnp.pad(region_map, ((tap_reach, tap_reach), (0, 0)), constant_values=-1)
    all_rows = lax.all_gather(planes, "row", axis=1, tiled=True)
    extended = jnp.pad(all_rows, ((0, 0), (tap_reach, tap_reach), (0, 0)))
    padded = build_taps(extended, region_padded)
    piece_width = point_spread.shape[3]
    partial_value = project(padded, point_spread[0], all_rows.shape[1])
    frames, total_rows, merged = partial_value.shape
    split_partial = partial_value.reshape(frames, total_rows, merged // piece_width, piece_width)
    returned = lax.all_to_all(split_partial, "row", split_axis=1, concat_axis=3, tiled=True)
    camera = returned.reshape(frames, row_count, returned.shape[2] * returned.shape[3])
    residual = pixel_weight.astype(jnp.float32) * (camera - measured.astype(jnp.float32))
    return (camera, residual)


def round_up(value, step):
    return (value + step - 1) // step * step


def remote(src, dst, send_sem, recv_sem, device):
    return pltpu.make_async_remote_copy(
        src_ref=src, dst_ref=dst, send_sem=send_sem, recv_sem=recv_sem,
        device_id=device, device_id_type=pl.DeviceIdType.MESH,
    )


def lanes_from_rows(raw, wide, pieces, vin):
    rows_here, phases, cols = vin.shape
    group = math.lcm(phases, 128) // phases
    span = group * phases
    groups = cols // group
    wide[:, span:] = jnp.zeros((wide.shape[0], wide.shape[1] - span), jnp.float32)
    for at in range(groups):
        strip = raw[:, at * span:(at + 1) * span].astype(jnp.float32)
        for row in range(rows_here):
            wide[row * groups + at:row * groups + at + 1, :span] = strip[row:row + 1]
    for member in range(group):
        for half in range(pieces.shape[0]):
            first = member * phases + half * 128
            pieces[half, pl.ds(member, rows_here * groups, stride=group), :] = wide[:, first:first + 128]
    for row in range(rows_here):
        for half in range(pieces.shape[0]):
            count = min(128, phases - half * 128)
            turned = pieces[half, row * cols:(row + 1) * cols, :].T
            vin[row, half * 128:half * 128 + count, :] = turned[:count].astype(jnp.bfloat16)


def kernel(frames, depths, row_shards, v_hbm, w_hbm, region, m_hbm, p_hbm, cam, res, raw, wide, pieces, vin,
           mraw, praw, in_sem, vol, wraw, wflat, xmask, part, xrecv, zsend,
           zrecv, yred, fin, w_sem, g_send, g_recv, x_send, x_recv, z_send, z_recv, y_send, y_recv):
    reach = TAP_SIDE // 2
    rows_here, phases, cols = vin.shape
    rows = rows_here * row_shards
    taps, width, depth_rows = w_hbm.shape
    blocks_here = depth_rows // phases
    stride = wflat.shape[0] // TAP_SIDE
    qpad = part.shape[3]
    col_share = cols // depths
    quads = rows // depths
    me_f, me_d, me_r = lax.axis_index("frame"), lax.axis_index("depth"), lax.axis_index("row")
    other_f = 1 - me_f
    core_r = me_r + 1 - 2 * lax.rem(me_r, 2)
    far_r = lax.rem(me_r + 2, row_shards)
    far_core_r = far_r + 1 - 2 * lax.rem(far_r, 2)


    x_dev = (other_f, me_d, me_r)
    core_dev = (me_f, me_d, core_r)
    far_dev = (me_f, me_d, far_r)
    diag_dev = (other_f, me_d, far_r)
    partners = [x_dev, diag_dev]
    partners += [(me_f, me_d, lax.rem(me_r + step, row_shards)) for step in range(1, row_shards)]
    partners += [(me_f, lax.rem(me_d + step, depths), me_r) for step in range(1, depths)]
    barrier = pltpu.get_barrier_semaphore()
    for device in partners:
        pl.semaphore_signal(barrier, inc=1, device_id=device, device_id_type=pl.DeviceIdType.MESH)
    v_copy = pltpu.make_async_copy(v_hbm, raw, in_sem.at[0])
    v_copy.start()
    w_copy = pltpu.make_async_copy(w_hbm, wraw, w_sem)
    w_copy.start()
    m_copy = pltpu.make_async_copy(m_hbm, mraw, in_sem.at[1])
    m_copy.start()
    p_copy = pltpu.make_async_copy(p_hbm, praw, in_sem.at[2])
    p_copy.start()
    v_copy.wait()
    lanes_from_rows(raw, wide, pieces, vin)
    pl.semaphore_wait(barrier, len(partners))

    def slot(frame, row):
        return vol.at[frame, pl.ds(row * rows_here, rows_here)]

    def gather(index, src, frame, row, device):
        return remote(src, slot(frame, row), g_send.at[index], g_recv.at[index], device)

    own_x = gather(0, vin, me_f, me_r, x_dev)
    own_far = gather(1, vin, me_f, me_r, far_dev)
    own_diag = gather(2, vin, me_f, me_r, diag_dev)
    own_core = gather(3, vin, me_f, me_r, core_dev)
    for copy in (own_x, own_far, own_diag, own_core):
        copy.start()
    slot(me_f, me_r)[...] = vin[...]

    w_copy.wait()
    for tap_col in range(TAP_SIDE):
        bands = [wraw[(TAP_SIDE - 1 - at) * TAP_SIDE + tap_col] for at in range(TAP_SIDE)]
        wflat[tap_col * stride:tap_col * stride + width, :] = jnp.concatenate(bands, axis=1)
    edge = jnp.zeros((reach * depth_rows, frames * cols), jnp.bfloat16)
    xmask[:reach * depth_rows, :] = edge
    xmask[(rows + reach) * depth_rows:, :] = edge

    own_x.wait_recv()
    fwd_x = gather(4, slot(other_f, me_r), other_f, me_r, core_dev)
    fwd_x.start()
    own_far.wait_recv()
    fwd_far = gather(5, slot(me_f, far_r), me_f, far_r, core_dev)
    fwd_far.start()
    own_diag.wait_recv()
    fwd_diag = gather(6, slot(other_f, far_r), other_f, far_r, core_dev)
    fwd_diag.start()
    for copy in (own_core, fwd_x, fwd_far, fwd_diag):
        copy.wait_recv()

    first_block = me_f * blocks_here
    for row in range(rows):
        for block in range(blocks_here):
            keep = (region[row:row + 1, :] == first_block + block).astype(jnp.float32).astype(jnp.bfloat16)
            top = (row + reach) * depth_rows + block * phases
            for frame in range(frames):
                xmask[top:top + phases, frame * cols:(frame + 1) * cols] = vol[frame, row] * keep

    lane = lax.broadcasted_iota(jnp.int32, (qpad, cols), 1)
    order = sorted(range(1, depths), key=lambda step: abs(step - depths // 2))
    x_copies, z_copies = {}, {}

    def frame_copy(quad, step):
        share = lax.rem(me_d + step, depths)
        return remote(part.at[other_f, quad, share], xrecv.at[quad, share], x_send.at[quad, step],
                      x_recv.at[quad, step], x_dev)

    for quad in range(quads):
        sums = [[None] * frames for _ in range(depths)]
        for at in range(depths):
            row = quad * depths + at
            slab = xmask[row * depth_rows:(row + TAP_SIDE) * depth_rows, :]
            product = jnp.dot(wflat[...], slab, preferred_element_type=jnp.float32)
            for frame in range(frames):
                total = None
                for tap_col in range(TAP_SIDE):
                    shift = tap_col - reach
                    piece = product[tap_col * stride:tap_col * stride + qpad, frame * cols:(frame + 1) * cols]
                    if shift:
                        piece = pltpu.roll(piece, shift % cols, 1)
                        inside = lane >= shift if shift > 0 else lane < cols + shift
                        piece = jnp.where(inside, piece, 0.0)
                    total = piece if total is None else total + piece
                sums[at][frame] = total
        for frame in range(frames):
            for share in range(depths):
                packed = None
                for at in range(depths):
                    shift = (at - share) * col_share % cols
                    moved = pltpu.roll(sums[at][frame], shift, 1) if shift else sums[at][frame]
                    packed = moved if packed is None else jnp.where(lane >= at * col_share, moved, packed)
                part[frame, quad, share] = packed
        for step in order:
            x_copies[quad, step] = frame_copy(quad, step)
            x_copies[quad, step].start()

    for quad in range(quads):
        x_copies[quad, 0] = frame_copy(quad, 0)
        x_copies[quad, 0].start()
    for quad in range(quads):
        for step in order:
            to = lax.rem(me_d + step, depths)
            x_copies[quad, step].wait_recv()
            zsend[quad, to] = part[me_f, quad, to] + xrecv[quad, to]
            z_copies[quad, step] = remote(zsend.at[quad, to], zrecv.at[quad, step - 1], z_send.at[quad, step - 1],
                                          z_recv.at[quad, step - 1], (me_f, to, me_r))
            z_copies[quad, step].start()
    shares = row_shards // quads

    def row_copy(to):
        return remote(yred.at[to // shares], fin.at[me_r], y_send.at[to], y_recv.at[me_r], (me_f, me_d, to))

    for quad in range(quads):
        x_copies[quad, 0].wait_recv()
        total = part[me_f, quad, me_d] + xrecv[quad, me_d]
        for step in order:
            z_copies[quad, step].wait_recv()
            total = total + zrecv[quad, step - 1]
        yred[quad] = total
        for to in range(quad * shares, (quad + 1) * shares):
            @pl.when(to != me_r)
            def _():
                row_copy(to).start()
    fin[me_r] = yred[me_r // shares]
    for source in range(row_shards):
        @pl.when(source != me_r)
        def _():
            remote(yred.at[0], fin.at[source], y_send.at[source], y_recv.at[source],
                   (me_f, me_d, source)).wait_recv()
            row_copy(source).wait_send()
    lanes_here = rows_here * col_share
    back = lax.rem(cols - lax.rem(me_r, shares) * lanes_here, cols)
    turned = jnp.concatenate(
        [pltpu.roll(fin[source], back, 1).T[:lanes_here, :width] for source in range(row_shards)], axis=1
    )
    halves = pieces.shape[0]
    for half in range(halves):
        count = min(128, phases - half * 128)
        pieces[half, :lanes_here, :count] = turned[:, half * 128:half * 128 + count]
    group = math.lcm(phases, 128) // phases
    span = group * phases
    per_row = col_share // group
    members = []
    for member in range(group):
        for half in range(halves):
            count = min(128, phases - half * 128)
            members.append(pieces[half, pl.ds(member, rows_here * per_row, stride=group), :][:, :count])
    strips = jnp.concatenate(members, axis=1)
    for row in range(rows_here):
        for at in range(per_row):
            line = row * per_row + at
            cam[row:row + 1, at * span:(at + 1) * span] = strips[line:line + 1]
    m_copy.wait()
    p_copy.wait()
    res[...] = praw[...].astype(jnp.float32) * (cam[...] - mraw[...].astype(jnp.float32))
    for copy in (own_x, own_far, own_diag, own_core, fwd_x, fwd_far, fwd_diag, *x_copies.values(), *z_copies.values()):
        copy.wait_send()


def hand_over(camera_in, residual_in, camera_out, residual_out):
    camera_out[...] = camera_in[...]
    residual_out[...] = residual_in[...]


def fused_body(sizes, volume, point_spread, region_map, measured, pixel_weight):
    frames, depths, row_shards = sizes
    _, _, rows_here, merged = volume.shape
    cols = merged // PHASES
    _, depth_rows, taps, width = point_spread.shape
    rows = rows_here * row_shards
    quads = rows // depths
    qpad = width
    stride = round_up(width, 16)
    group = math.lcm(PHASES, 128) // PHASES
    span = group * PHASES
    image = (rows_here, cols // depths * PHASES)
    spread = point_spread.reshape(depth_rows, taps, width).transpose(1, 2, 0)
    vmem = pl.BlockSpec(memory_space=pltpu.VMEM)
    hbm = pl.BlockSpec(memory_space=pl.ANY)
    dma = pltpu.SemaphoreType.DMA
    camera, residual = pl.pallas_call(
        functools.partial(kernel, frames, depths, row_shards),
        out_shape=[jax.ShapeDtypeStruct(image, jnp.float32)] * 2,
        in_specs=[hbm, hbm, vmem, hbm, hbm],
        out_specs=[vmem, vmem],
        scratch_shapes=[
            pltpu.VMEM((rows_here, merged), jnp.bfloat16),
            pltpu.VMEM((rows_here * cols // group, span + 128), jnp.float32),
            pltpu.VMEM((round_up(PHASES, 128) // 128, rows_here * cols, 128), jnp.float32),
            pltpu.VMEM((rows_here, PHASES, cols), jnp.bfloat16),
            pltpu.VMEM(image, jnp.bfloat16),
            pltpu.VMEM(image, jnp.int32),
            dma((3,)),
            pltpu.VMEM((frames, rows, PHASES, cols), jnp.bfloat16),
            pltpu.VMEM((taps, width, depth_rows), jnp.bfloat16),
            pltpu.VMEM((TAP_SIDE * stride, TAP_SIDE * depth_rows), jnp.bfloat16),
            pltpu.VMEM(((rows + TAP_SIDE - 1) * depth_rows, frames * cols), jnp.bfloat16),
            pltpu.VMEM((frames, quads, depths, qpad, cols), jnp.float32),
            pltpu.VMEM((quads, depths, qpad, cols), jnp.float32),
            pltpu.VMEM((quads, depths, qpad, cols), jnp.float32),
            pltpu.VMEM((quads, depths - 1, qpad, cols), jnp.float32),
            pltpu.VMEM((quads, qpad, cols), jnp.float32),
            pltpu.VMEM((row_shards, qpad, cols), jnp.float32),
            dma, dma((7,)), dma((7,)), dma((quads, depths)), dma((quads, depths)),
            dma((quads, depths - 1)), dma((quads, depths - 1)),
            dma((row_shards,)), dma((row_shards,)),
        ],
        compiler_params=pltpu.CompilerParams(collective_id=0, has_side_effects=True),
    )(volume.reshape(rows_here, merged), spread, region_map, measured.reshape(image), pixel_weight.reshape(image))
    camera, residual = pl.pallas_call(
        hand_over,
        out_shape=[jax.ShapeDtypeStruct(image, jnp.float32)] * 2,
        in_specs=[vmem, vmem],
        out_specs=[vmem, vmem],
    )(camera, residual)
    return (camera.reshape(measured.shape), residual.reshape(measured.shape))


def solution(mesh):
    in_specs = (
        P("depth", "frame", "row", None),
        P("depth", "frame", None, "row"),
        P(),
        P("frame", "row", "depth"),
        P("frame", "row", "depth"),
    )
    out_specs = (P("frame", "row", "depth"), P("frame", "row", "depth"))
    sizes = (mesh.shape["frame"], mesh.shape["depth"], mesh.shape["row"])

    def body(volume, *rest):
        rows = volume.shape[2] * sizes[2]
        blocks_fit = rest[0].shape[1] % PHASES == 0
        quads = rows // sizes[1] if rows % sizes[1] == 0 else 0
        packs = quads and sizes[2] % quads == 0 and (volume.shape[3] // PHASES) == 128
        if sizes[0] == 2 and sizes[2] == 4 and volume.shape[1] == 1 and blocks_fit and packs:
            return fused_body(sizes, volume, *rest)
        return plain_body(volume, *rest)

    return jax.shard_map(body, mesh=mesh, in_specs=in_specs, out_specs=out_specs, check_vma=False)
```

```python
import functools
import math

import jax
import jax.numpy as jnp
from jax import lax
from jax.experimental import pallas as pl
from jax.experimental.pallas import tpu as pltpu
from jax.sharding import PartitionSpec as P

PHASES = 144
BLOCKS = 4
TAP_SIDE = 5


def build_taps(planes, region_rows):
    tap_reach = TAP_SIDE // 2
    frames, row_count, merged = planes.shape
    col_count = merged // PHASES
    split_planes = planes.reshape(frames, row_count, col_count, PHASES)
    block_ids = jnp.arange(BLOCKS, dtype=jnp.int32)
    onehot = (region_rows[:, :, None] == block_ids[None, None, :]).astype(jnp.bfloat16)
    expanded = (split_planes[:, :, :, None, :] * onehot[None, :, :, :, None]).reshape(
        frames, row_count, col_count, BLOCKS * PHASES
    )
    return jnp.pad(expanded, ((0, 0), (0, 0), (tap_reach, tap_reach), (0, 0)))


def project(padded, spread_local, out_rows):
    tap_reach = TAP_SIDE // 2
    frames, ext_rows, ext_cols, _ = padded.shape
    col_count = ext_cols - 2 * tap_reach
    out_width = spread_local.shape[2]
    zero_start = jnp.zeros((frames * out_rows * col_count, out_width), jnp.float32)
    running = zero_start
    spread_slab = lax.all_gather(spread_local, "frame", axis=0, tiled=True)
    piece_rows = spread_slab.shape[0]
    flat_cols = padded.reshape(frames * ext_rows * ext_cols, piece_rows)
    for tap_row in range(TAP_SIDE):
        row_taps = spread_slab[:, tap_row * TAP_SIDE : (tap_row + 1) * TAP_SIDE, :].reshape(
            piece_rows, TAP_SIDE * out_width
        )
        product = jnp.dot(flat_cols, row_taps, preferred_element_type=jnp.float32)
        product = product.reshape(frames, ext_rows, ext_cols, TAP_SIDE, out_width)
        first_row = 2 * tap_reach - tap_row
        for tap_col in range(TAP_SIDE):
            first_col = 2 * tap_reach - tap_col
            shifted = product[
                :, first_row : first_row + out_rows, first_col : first_col + col_count, tap_col, :
            ]
            running = running + shifted.reshape(frames * out_rows * col_count, out_width)
    partial_value = running.reshape(frames, out_rows, col_count * out_width)
    return lax.psum_scatter(partial_value, "depth", scatter_dimension=2, tiled=True)


def plain_body(volume, point_spread, region_map, measured, pixel_weight):
    tap_reach = TAP_SIDE // 2
    planes = volume[0]
    row_count = planes.shape[1]
    region_padded = jnp.pad(region_map, ((tap_reach, tap_reach), (0, 0)), constant_values=-1)
    all_rows = lax.all_gather(planes, "row", axis=1, tiled=True)
    extended = jnp.pad(all_rows, ((0, 0), (tap_reach, tap_reach), (0, 0)))
    padded = build_taps(extended, region_padded)
    piece_width = point_spread.shape[3]
    partial_value = project(padded, point_spread[0], all_rows.shape[1])
    frames, total_rows, merged = partial_value.shape
    split_partial = partial_value.reshape(frames, total_rows, merged // piece_width, piece_width)
    returned = lax.all_to_all(split_partial, "row", split_axis=1, concat_axis=3, tiled=True)
    camera = returned.reshape(frames, row_count, returned.shape[2] * returned.shape[3])
    residual = pixel_weight.astype(jnp.float32) * (camera - measured.astype(jnp.float32))
    return (camera, residual)


def round_up(value, step):
    return (value + step - 1) // step * step


def remote(src, dst, send_sem, recv_sem, device):
    return pltpu.make_async_remote_copy(
        src_ref=src, dst_ref=dst, send_sem=send_sem, recv_sem=recv_sem,
        device_id=device, device_id_type=pl.DeviceIdType.MESH,
    )


def lanes_from_rows(raw, wide, pieces, vin):
    rows_here, phases, cols = vin.shape
    group = math.lcm(phases, 128) // phases
    span = group * phases
    groups = cols // group
    wide[:, span:] = jnp.zeros((wide.shape[0], wide.shape[1] - span), jnp.float32)
    for at in range(groups):
        strip = raw[:, at * span:(at + 1) * span].astype(jnp.float32)
        for row in range(rows_here):
            wide[row * groups + at:row * groups + at + 1, :span] = strip[row:row + 1]
    for member in range(group):
        for half in range(pieces.shape[0]):
            first = member * phases + half * 128
            pieces[half, pl.ds(member, rows_here * groups, stride=group), :] = wide[:, first:first + 128]
    for row in range(rows_here):
        for half in range(pieces.shape[0]):
            count = min(128, phases - half * 128)
            turned = pieces[half, row * cols:(row + 1) * cols, :].T
            vin[row, half * 128:half * 128 + count, :] = turned[:count].astype(jnp.bfloat16)


def kernel(frames, depths, row_shards, v_hbm, w_hbm, region, cam, raw, wide, pieces, vin,
           in_sem, vol, wraw, wflat, xmask, part, xrecv, zsend,
           zrecv, yred, fin, w_sem, g_send, g_recv, x_send, x_recv, z_send, z_recv, y_send, y_recv):
    reach = TAP_SIDE // 2
    rows_here, phases, cols = vin.shape
    rows = rows_here * row_shards
    taps, width, depth_rows = w_hbm.shape
    blocks_here = depth_rows // phases
    stride = wflat.shape[0] // TAP_SIDE
    qpad = part.shape[3]
    col_share = cols // depths
    quads = rows // depths
    me_f, me_d, me_r = lax.axis_index("frame"), lax.axis_index("depth"), lax.axis_index("row")
    other_f = 1 - me_f
    core_r = me_r + 1 - 2 * lax.rem(me_r, 2)
    far_r = lax.rem(me_r + 2, row_shards)
    far_core_r = far_r + 1 - 2 * lax.rem(far_r, 2)


    x_dev = (other_f, me_d, me_r)
    core_dev = (me_f, me_d, core_r)
    far_dev = (me_f, me_d, far_r)
    diag_dev = (other_f, me_d, far_r)
    partners = [x_dev, diag_dev]
    partners += [(me_f, me_d, lax.rem(me_r + step, row_shards)) for step in range(1, row_shards)]
    partners += [(me_f, lax.rem(me_d + step, depths), me_r) for step in range(1, depths)]
    barrier = pltpu.get_barrier_semaphore()
    for device in partners:
        pl.semaphore_signal(barrier, inc=1, device_id=device, device_id_type=pl.DeviceIdType.MESH)
    v_copy = pltpu.make_async_copy(v_hbm, raw, in_sem.at[0])
    v_copy.start()
    w_copy = pltpu.make_async_copy(w_hbm, wraw, w_sem)
    w_copy.start()
    v_copy.wait()
    lanes_from_rows(raw, wide, pieces, vin)
    pl.semaphore_wait(barrier, len(partners))

    def slot(frame, row):
        return vol.at[frame, pl.ds(row * rows_here, rows_here)]

    def gather(index, src, frame, row, device):
        return remote(src, slot(frame, row), g_send.at[index], g_recv.at[index], device)

    own_x = gather(0, vin, me_f, me_r, x_dev)
    own_far = gather(1, vin, me_f, me_r, far_dev)
    own_diag = gather(2, vin, me_f, me_r, diag_dev)
    own_core = gather(3, vin, me_f, me_r, core_dev)
    for copy in (own_x, own_far, own_diag, own_core):
        copy.start()
    slot(me_f, me_r)[...] = vin[...]

    w_copy.wait()
    for tap_col in range(TAP_SIDE):
        bands = [wraw[(TAP_SIDE - 1 - at) * TAP_SIDE + tap_col] for at in range(TAP_SIDE)]
        wflat[tap_col * stride:tap_col * stride + width, :] = jnp.concatenate(bands, axis=1)
    edge = jnp.zeros((reach * depth_rows, frames * cols), jnp.bfloat16)
    xmask[:reach * depth_rows, :] = edge
    xmask[(rows + reach) * depth_rows:, :] = edge

    own_x.wait_recv()
    fwd_x = gather(4, slot(other_f, me_r), other_f, me_r, core_dev)
    fwd_x.start()
    own_far.wait_recv()
    fwd_far = gather(5, slot(me_f, far_r), me_f, far_r, core_dev)
    fwd_far.start()
    own_diag.wait_recv()
    fwd_diag = gather(6, slot(other_f, far_r), other_f, far_r, core_dev)
    fwd_diag.start()
    for copy in (own_core, fwd_x, fwd_far, fwd_diag):
        copy.wait_recv()

    first_block = me_f * blocks_here
    for row in range(rows):
        for block in range(blocks_here):
            keep = (region[row:row + 1, :] == first_block + block).astype(jnp.float32).astype(jnp.bfloat16)
            top = (row + reach) * depth_rows + block * phases
            for frame in range(frames):
                xmask[top:top + phases, frame * cols:(frame + 1) * cols] = vol[frame, row] * keep

    lane = lax.broadcasted_iota(jnp.int32, (qpad, cols), 1)
    order = sorted(range(1, depths), key=lambda step: abs(step - depths // 2))
    x_copies, z_copies = {}, {}

    def frame_copy(quad, step):
        share = lax.rem(me_d + step, depths)
        return remote(part.at[other_f, quad, share], xrecv.at[quad, share], x_send.at[quad, step],
                      x_recv.at[quad, step], x_dev)

    for quad in range(quads):
        sums = [[None] * frames for _ in range(depths)]
        for at in range(depths):
            row = quad * depths + at
            slab = xmask[row * depth_rows:(row + TAP_SIDE) * depth_rows, :]
            product = jnp.dot(wflat[...], slab, preferred_element_type=jnp.float32)
            for frame in range(frames):
                total = None
                for tap_col in range(TAP_SIDE):
                    shift = tap_col - reach
                    piece = product[tap_col * stride:tap_col * stride + qpad, frame * cols:(frame + 1) * cols]
                    if shift:
                        piece = pltpu.roll(piece, shift % cols, 1)
                        inside = lane >= shift if shift > 0 else lane < cols + shift
                        piece = jnp.where(inside, piece, 0.0)
                    total = piece if total is None else total + piece
                sums[at][frame] = total
        for frame in range(frames):
            for share in range(depths):
                packed = None
                for at in range(depths):
                    shift = (at - share) * col_share % cols
                    moved = pltpu.roll(sums[at][frame], shift, 1) if shift else sums[at][frame]
                    packed = moved if packed is None else jnp.where(lane >= at * col_share, moved, packed)
                part[frame, quad, share] = packed
        for step in order:
            x_copies[quad, step] = frame_copy(quad, step)
            x_copies[quad, step].start()

    for quad in range(quads):
        x_copies[quad, 0] = frame_copy(quad, 0)
        x_copies[quad, 0].start()
    for quad in range(quads):
        for step in order:
            to = lax.rem(me_d + step, depths)
            x_copies[quad, step].wait_recv()
            zsend[quad, to] = part[me_f, quad, to] + xrecv[quad, to]
            z_copies[quad, step] = remote(zsend.at[quad, to], zrecv.at[quad, step - 1], z_send.at[quad, step - 1],
                                          z_recv.at[quad, step - 1], (me_f, to, me_r))
            z_copies[quad, step].start()
    shares = row_shards // quads

    def row_copy(to):
        return remote(yred.at[to // shares], fin.at[me_r], y_send.at[to], y_recv.at[me_r], (me_f, me_d, to))

    for quad in range(quads):
        x_copies[quad, 0].wait_recv()
        total = part[me_f, quad, me_d] + xrecv[quad, me_d]
        for step in order:
            z_copies[quad, step].wait_recv()
            total = total + zrecv[quad, step - 1]
        yred[quad] = total
        for to in range(quad * shares, (quad + 1) * shares):
            @pl.when(to != me_r)
            def _():
                row_copy(to).start()
    fin[me_r] = yred[me_r // shares]
    for source in range(row_shards):
        @pl.when(source != me_r)
        def _():
            remote(yred.at[0], fin.at[source], y_send.at[source], y_recv.at[source],
                   (me_f, me_d, source)).wait_recv()
            row_copy(source).wait_send()
    lanes_here = rows_here * col_share
    back = lax.rem(cols - lax.rem(me_r, shares) * lanes_here, cols)
    turned = jnp.concatenate(
        [pltpu.roll(fin[source], back, 1).T[:lanes_here, :width] for source in range(row_shards)], axis=1
    )
    halves = pieces.shape[0]
    for half in range(halves):
        count = min(128, phases - half * 128)
        pieces[half, :lanes_here, :count] = turned[:, half * 128:half * 128 + count]
    group = math.lcm(phases, 128) // phases
    span = group * phases
    per_row = col_share // group
    members = []
    for member in range(group):
        for half in range(halves):
            count = min(128, phases - half * 128)
            members.append(pieces[half, pl.ds(member, rows_here * per_row, stride=group), :][:, :count])
    strips = jnp.concatenate(members, axis=1)
    for row in range(rows_here):
        for at in range(per_row):
            line = row * per_row + at
            cam[row:row + 1, at * span:(at + 1) * span] = strips[line:line + 1]
    for copy in (own_x, own_far, own_diag, own_core, fwd_x, fwd_far, fwd_diag, *x_copies.values(), *z_copies.values()):
        copy.wait_send()


def hand_over(camera_in, recorded, weight, camera_out, residual_out):
    camera_out[...] = camera_in[...]
    residual_out[...] = weight[...].astype(jnp.float32) * (camera_in[...] - recorded[...].astype(jnp.float32))


def fused_body(sizes, volume, point_spread, region_map, measured, pixel_weight):
    frames, depths, row_shards = sizes
    _, _, rows_here, merged = volume.shape
    cols = merged // PHASES
    _, depth_rows, taps, width = point_spread.shape
    rows = rows_here * row_shards
    quads = rows // depths
    qpad = width
    stride = round_up(width, 16)
    group = math.lcm(PHASES, 128) // PHASES
    span = group * PHASES
    image = (rows_here, cols // depths * PHASES)
    spread = point_spread.reshape(depth_rows, taps, width).transpose(1, 2, 0)
    vmem = pl.BlockSpec(memory_space=pltpu.VMEM)
    hbm = pl.BlockSpec(memory_space=pl.ANY)
    dma = pltpu.SemaphoreType.DMA
    camera = pl.pallas_call(
        functools.partial(kernel, frames, depths, row_shards),
        out_shape=jax.ShapeDtypeStruct(image, jnp.float32),
        in_specs=[hbm, hbm, vmem],
        out_specs=vmem,
        scratch_shapes=[
            pltpu.VMEM((rows_here, merged), jnp.bfloat16),
            pltpu.VMEM((rows_here * cols // group, span + 128), jnp.float32),
            pltpu.VMEM((round_up(PHASES, 128) // 128, rows_here * cols, 128), jnp.float32),
            pltpu.VMEM((rows_here, PHASES, cols), jnp.bfloat16),
            dma((1,)),
            pltpu.VMEM((frames, rows, PHASES, cols), jnp.bfloat16),
            pltpu.VMEM((taps, width, depth_rows), jnp.bfloat16),
            pltpu.VMEM((TAP_SIDE * stride, TAP_SIDE * depth_rows), jnp.bfloat16),
            pltpu.VMEM(((rows + TAP_SIDE - 1) * depth_rows, frames * cols), jnp.bfloat16),
            pltpu.VMEM((frames, quads, depths, qpad, cols), jnp.float32),
            pltpu.VMEM((quads, depths, qpad, cols), jnp.float32),
            pltpu.VMEM((quads, depths, qpad, cols), jnp.float32),
            pltpu.VMEM((quads, depths - 1, qpad, cols), jnp.float32),
            pltpu.VMEM((quads, qpad, cols), jnp.float32),
            pltpu.VMEM((row_shards, qpad, cols), jnp.float32),
            dma, dma((7,)), dma((7,)), dma((quads, depths)), dma((quads, depths)),
            dma((quads, depths - 1)), dma((quads, depths - 1)),
            dma((row_shards,)), dma((row_shards,)),
        ],
        compiler_params=pltpu.CompilerParams(collective_id=0, has_side_effects=True),
    )(volume.reshape(rows_here, merged), spread, region_map)
    camera, residual = pl.pallas_call(
        hand_over,
        out_shape=[jax.ShapeDtypeStruct(image, jnp.float32)] * 2,
        in_specs=[vmem] * 3,
        out_specs=[vmem, vmem],
    )(camera, measured.reshape(image), pixel_weight.reshape(image))
    return (camera.reshape(measured.shape), residual.reshape(measured.shape))


def solution(mesh):
    in_specs = (
        P("depth", "frame", "row", None),
        P("depth", "frame", None, "row"),
        P(),
        P("frame", "row", "depth"),
        P("frame", "row", "depth"),
    )
    out_specs = (P("frame", "row", "depth"), P("frame", "row", "depth"))
    sizes = (mesh.shape["frame"], mesh.shape["depth"], mesh.shape["row"])

    def body(volume, *rest):
        rows = volume.shape[2] * sizes[2]
        blocks_fit = rest[0].shape[1] % PHASES == 0
        quads = rows // sizes[1] if rows % sizes[1] == 0 else 0
        packs = quads and sizes[2] % quads == 0 and (volume.shape[3] // PHASES) == 128
        if sizes[0] == 2 and sizes[2] == 4 and volume.shape[1] == 1 and blocks_fit and packs:
            return fused_body(sizes, volume, *rest)
        return plain_body(volume, *rest)

    return jax.shard_map(body, mesh=mesh, in_specs=in_specs, out_specs=out_specs, check_vma=False)
```
